512 devices in a mesh: seq: 64 (over y, z), head: 8 (over x, core).
Axes of the slice: x: 4, y: 8, z: 8, core: 2. Of those that a mesh axis runs over, the one named last changes fastest.
Arguments:
- queries: bfloat16 [16384, 1024], P('seq', 'head'), may hold values from -5 to 5
- key_rows: bfloat16 [16384, 1024], P('seq', 'head'), may hold values from -5 to 5
- value_rows: bfloat16 [16384, 1024], P('seq', 'head'), may hold values from -6 to 6
- key_blocks: int32 [256, 9], P('seq'), may hold values from -1 to 254, as said below
- out_weight: bfloat16 [1024, 1024], P('head'), may hold values from -0.1875 to 0.1875
- grad_out: bfloat16 [16384, 1024], P('seq', 'head'), may hold values from -6 to 6
Outputs:
- mixed: bfloat16 [16384, 1024], P('seq', 'head')
- grad_queries: bfloat16 [16384, 1024], P('seq', 'head')
- grad_keys: bfloat16 [16384, 1024], P('seq', 'head')
- grad_values: bfloat16 [16384, 1024], P('seq', 'head')
The draws below stay inside these ranges and needn't reach their ends.
Inputs may be any that keep to these rules, and one draw needn't show every extreme that they name: key_blocks[q, j] is either q - 2**j or -1; it is -1 wherever q < 2**j, and never -1 for j = 0 and q >= 1.
All inputs are finite; a program needn't handle non-finite values.
Results may differ from the reference program's by a relative error of at most 0.03.
Values may be sent and summed in bfloat16 or wider, within the bound.
A program may use at most 64 MiB of HBM per device.

```python
import jax
import jax.numpy as jnp
from jax import lax

D = 1024
HD = 128
BLOCK = 64
LEVELS = 9
HEADS = 8
WIDTH = 1024
TOKENS = 16384
BLOCKS_ALL = 256
N_HEAD = 8


def drawn(key):
    width = HEADS * HD
    query_key, key_key = jax.random.split(jax.random.fold_in(key, 11), 2)
    query_base = jnp.clip(jax.random.normal(query_key, (TOKENS, width), jnp.float32), -4.0, 4.0)
    key_base = jnp.clip(jax.random.normal(key_key, (TOKENS, width), jnp.float32), -4.0, 4.0)
    return (query_base, key_base)


def draw_queries(key, part):
    return drawn(key)[0].astype(jnp.bfloat16)


def draw_key_rows(key, part):
    return drawn(key)[1].astype(jnp.bfloat16)


def draw_key_blocks(key, part):
    kept = jax.random.randint(jax.random.fold_in(key, 23), (BLOCKS_ALL, LEVELS), 0, 4)
    blocks = jnp.arange(BLOCKS_ALL, dtype=jnp.int32)[:, None]
    powers = (2 ** jnp.arange(LEVELS, dtype=jnp.int32))[None, :]
    first = jnp.arange(LEVELS, dtype=jnp.int32)[None, :] == 0
    valid = (blocks >= powers) & ((kept > 0) | first)
    return jnp.where(valid, blocks - powers, -1).astype(jnp.int32)


def block_levels(rng, shape, pieces, least, high):
    factor_of, own = 1.0, jax.random.fold_in(rng, 6)
    for dim, blocks in pieces:
        draws = jnp.exp(jax.random.uniform(jax.random.fold_in(own, dim), (blocks,), jnp.float32, least / len(pieces), high / len(pieces)))
        factor_of = factor_of * jnp.repeat(draws, shape[dim] // blocks).reshape([-1 if axis == dim else 1 for axis in range(len(shape))])
    return factor_of


def scatter_about(own_key, shape, scale, most, shards=(), held_as=jnp.bfloat16):
    values = scale * jax.random.normal(own_key, shape, jnp.float32)
    if shards:
        values = values * block_levels(own_key, shape, shards, -0.22, 0.18)
    return jnp.clip(values, -most, most).astype(held_as)


def setup_inputs(seed: int = 0) -> dict:
    key_of = jax.random.split(jax.random.key(seed), 7)
    queries = draw_queries(jax.random.fold_in(key_of[6], 71), 0)
    key_rows = draw_key_rows(jax.random.fold_in(key_of[6], 71), 0)
    value_rows = scatter_about(key_of[2], (TOKENS, WIDTH), 1.0, 6.0, ((0, 64), (1, 8)))
    key_blocks = draw_key_blocks(jax.random.fold_in(key_of[6], 71), 0)
    out_weight = scatter_about(key_of[4], (WIDTH, D), WIDTH ** -0.5, 0.1875, ((0, 8),))
    grad_out = scatter_about(key_of[5], (TOKENS, D), 1.0, 6.0, ((0, 64), (1, 8)))
    return dict(queries=queries, key_rows=key_rows, value_rows=value_rows, key_blocks=key_blocks, out_weight=out_weight, grad_out=grad_out)


def head_pass(query_head, key_head, value_head, grad_head, key_blocks):
    block_total = query_head.shape[0] // BLOCK
    scaling = HD ** -0.5
    indices = jnp.where(key_blocks >= 0, key_blocks, 0).astype(jnp.int32)

    def to_blocks(array):
        return array.reshape(block_total, BLOCK, HD).astype(jnp.float32)

    key_blk = to_blocks(key_head)
    value_blk = to_blocks(value_head)
    key_all = jnp.concatenate([key_blk[:, None], key_blk[indices]], axis=1)
    value_all = jnp.concatenate([value_blk[:, None], value_blk[indices]], axis=1)
    query_blk = to_blocks(query_head)
    grad_blk = to_blocks(grad_head)
    scores = jnp.einsum("qid,qlkd->qilk", query_blk, key_all) * scaling
    causal = jnp.arange(BLOCK)[:, None] >= jnp.arange(BLOCK)[None, :]
    diag_mask = jnp.broadcast_to(causal[None, :, None, :], (block_total, BLOCK, 1, BLOCK))
    level_mask = jnp.broadcast_to((key_blocks >= 0)[:, None, :, None], (block_total, BLOCK, LEVELS, BLOCK))
    allowed = jnp.concatenate([diag_mask, level_mask], axis=2)
    scores = jnp.where(allowed, scores, -1e30)
    highest = jnp.max(scores, axis=(2, 3), keepdims=True)
    log_total = highest + jnp.log(jnp.sum(jnp.exp(scores - highest), axis=(2, 3), keepdims=True))
    probs = jnp.exp(scores - log_total)
    probs_b = probs.astype(jnp.bfloat16).astype(jnp.float32)
    attn = jnp.einsum("qilk,qlkd->qid", probs_b, value_all).astype(jnp.bfloat16)
    row_inner = jnp.sum(grad_blk * attn.astype(jnp.float32), axis=-1)
    grad_probs = jnp.einsum("qid,qlkd->qilk", grad_blk, value_all)
    grad_scores = (probs * (grad_probs - row_inner[:, :, None, None]) * scaling).astype(jnp.bfloat16).astype(jnp.float32)
    grad_queries = jnp.einsum("qilk,qlkd->qid", grad_scores, key_all).astype(jnp.bfloat16)
    key_terms = jnp.einsum("qilk,qid->qlkd", grad_scores, query_blk)
    value_terms = jnp.einsum("qilk,qid->qlkd", probs_b, grad_blk)
    empty = jnp.zeros((block_total, BLOCK, HD), jnp.float32)
    grad_keys = (key_terms[:, 0] + empty.at[indices].add(key_terms[:, 1:])).astype(jnp.bfloat16)
    grad_values = (value_terms[:, 0] + empty.at[indices].add(value_terms[:, 1:])).astype(jnp.bfloat16)
    steps_all = block_total * BLOCK
    return (attn.reshape(steps_all, HD), grad_queries.reshape(steps_all, HD),
            grad_keys.reshape(steps_all, HD), grad_values.reshape(steps_all, HD))


def reference(queries, key_rows, value_rows, key_blocks, out_weight, grad_out):
    steps_all = queries.shape[0]
    head_total = queries.shape[1] // HD
    grad_attn = lax.dot_general(grad_out, out_weight, (((1,), (1,)), ((), ())),
                                preferred_element_type=jnp.float32).astype(jnp.bfloat16)

    def by_head(array):
        return array.reshape(steps_all, head_total, HD).transpose(1, 0, 2)

    def one_head(items):
        return head_pass(items[0], items[1], items[2], items[3], key_blocks)

    attn, grad_queries, grad_keys, grad_values = lax.map(
        one_head, (by_head(queries), by_head(key_rows), by_head(value_rows), by_head(grad_attn)))

    def merge_heads(array):
        return array.transpose(1, 0, 2).reshape(steps_all, head_total * HD)

    attn = merge_heads(attn)
    group_width = head_total * HD // N_HEAD

    def add_group(number, total):
        start = (number * group_width).astype(jnp.int32)
        attn_slice = lax.dynamic_slice_in_dim(attn, start, group_width, 1)
        weight_slice = lax.dynamic_slice_in_dim(out_weight, start, group_width, 0)
        partial_sum = jnp.dot(attn_slice, weight_slice, preferred_element_type=jnp.float32)
        rounded = lax.optimization_barrier(partial_sum.astype(jnp.bfloat16))
        return total + rounded.astype(jnp.float32)

    mixed = lax.fori_loop(0, N_HEAD, add_group, jnp.zeros((steps_all, out_weight.shape[1]), jnp.float32))
    return (mixed.astype(jnp.bfloat16), merge_heads(grad_queries),
            merge_heads(grad_keys), merge_heads(grad_values))
```

```python
import functools

import jax
import jax.numpy as jnp
from jax import lax
from jax.experimental import pallas as pl
from jax.experimental.pallas import tpu as pltpu
from jax.sharding import PartitionSpec as P

HD = 128
BLOCK = 64
LEVELS = 9
ROW_CHIPS = 8
MESH = pl.DeviceIdType.MESH
BIG = 1e30


def dot_nt(a, b):
    return lax.dot_general(a, b, (((1,), (1,)), ((), ())), preferred_element_type=jnp.float32)


def dot_nn(a, b):
    return lax.dot_general(a, b, (((1,), (0,)), ((), ())), preferred_element_type=jnp.float32)


def kernel(
    n_seq, n_head, dists,
    q_hbm, k_hbm, v_hbm, kb_ref, w_hbm, g_hbm,
    mixed_ref, dq_ref, dk_ref, dv_ref,
    k_all, v_all, q_all, g_all, g_full, w_own, w_col, a_full, stat_mine, stat_got,
    seq_send, seq_recv, head_send, head_recv, stat_send, stat_recv, load_sem,
):
    seq = lax.axis_index("seq")
    head = lax.axis_index("head")
    nb = q_hbm.shape[0]
    slot_of = {dist: 1 + number for number, dist in enumerate(dists)}
    n_dist = len(dists)
    starts = [dist for dist in dists if dist in (1, ROW_CHIPS)]
    stages = []
    for dist in starts:
        chain = [(dist, None, dist)]
        while chain[-1][0] * 2 in dists and chain[-1][0] * 2 not in starts:
            chain.append((chain[-1][0] * 2, chain[-1][0], chain[-1][0]))
        stages.append(chain)

    def seq_peer(delta):
        return (lax.rem(seq + (delta + n_seq), n_seq), head)

    def head_peer(delta):
        return (seq, lax.rem(head + delta, n_head))

    loads = [
        pltpu.make_async_copy(k_hbm, k_all.at[0], load_sem.at[0]),
        pltpu.make_async_copy(v_hbm, v_all.at[0], load_sem.at[1]),
        pltpu.make_async_copy(q_hbm, q_all.at[0], load_sem.at[2]),
        pltpu.make_async_copy(w_hbm, w_own, load_sem.at[3]),
        pltpu.make_async_copy(
            g_hbm, g_full.at[:, pl.ds(pl.multiple_of(head * HD, HD), HD)], load_sem.at[4]
        ),
        pltpu.make_async_copy(
            w_hbm.at[:, pl.ds(pl.multiple_of(head * HD, HD), HD)],
            w_col.at[pl.ds(pl.multiple_of(head * HD, HD), HD), :],
            load_sem.at[5],
        ),
    ]
    for load in loads:
        load.start()

    barrier = pltpu.get_barrier_semaphore()
    deltas = sorted({d % n_seq for d in dists} | {(-d) % n_seq for d in dists})
    for delta in deltas:
        pl.semaphore_signal(barrier, inc=1, device_id=seq_peer(delta), device_id_type=MESH)
    for delta in range(1, n_head):
        pl.semaphore_signal(barrier, inc=1, device_id=head_peer(delta), device_id_type=MESH)
    pl.semaphore_wait(barrier, len(deltas) + n_head - 1)

    def seq_copies(number, own, buffer, sign):
        copies = {}
        for chain in stages:
            for dist, source, hop in chain:
                index = number * n_dist + slot_of[dist] - 1
                copies[dist] = pltpu.make_async_remote_copy(
                    src_ref=own if source is None else buffer.at[slot_of[source]],
                    dst_ref=buffer.at[slot_of[dist]],
                    send_sem=seq_send.at[index],
                    recv_sem=seq_recv.at[index],
                    device_id=seq_peer(sign * hop),
                    device_id_type=MESH,
                )
        return copies

    k_copies = seq_copies(0, k_hbm, k_all, 1)
    v_copies = seq_copies(1, v_hbm, v_all, 1)
    q_copies = seq_copies(2, q_hbm, q_all, -1)
    g_copies = seq_copies(3, g_all.at[0], g_all, -1)

    def head_copies(number, source, target):
        return [
            pltpu.make_async_remote_copy(
                src_ref=source(lax.rem(head + delta, n_head)),
                dst_ref=target,
                send_sem=head_send.at[number * (n_head - 1) + delta - 1],
                recv_sem=head_recv.at[number * (n_head - 1) + delta - 1],
                device_id=head_peer(delta),
                device_id_type=MESH,
            )
            for delta in range(1, n_head)
        ]

    my_columns = pl.ds(pl.multiple_of(head * HD, HD), HD)
    out_copies = head_copies(0, lambda peer: g_hbm, g_full.at[:, my_columns])
    w_copies = head_copies(
        1,
        lambda peer: w_hbm.at[:, pl.ds(pl.multiple_of(peer * HD, HD), HD)],
        w_col.at[my_columns, :],
    )
    a_copies = head_copies(2, lambda peer: a_full.at[:, my_columns], a_full.at[:, my_columns])

    def launch(copies):
        for dist in starts:
            copies[dist].start()

    def relay(copies, depth):
        for chain in stages:
            if depth < len(chain):
                copies[chain[depth][0]].wait_recv()
            if depth + 1 < len(chain):
                copies[chain[depth + 1][0]].start()

    most = max(len(chain) for chain in stages)
    launch(k_copies)
    launch(q_copies)
    for copy in out_copies:
        copy.start()
    launch(v_copies)
    for copy in w_copies:
        copy.start()
    for depth in range(most - 1):
        relay(k_copies, depth)
        relay(q_copies, depth)
    for load in loads:
        load.wait()
    for copy in out_copies:
        copy.wait_recv()
    g_own = dot_nt(g_full[...], w_own[...]).astype(jnp.bfloat16)
    for block in range(nb):
        g_all[0, block] = g_own[block * BLOCK : (block + 1) * BLOCK]
    launch(g_copies)
    for depth in range(most - 1):
        relay(v_copies, depth)
        relay(g_copies, depth)
    relay(k_copies, most - 1)
    relay(v_copies, most - 1)

    near = [2**power for power in range(LEVELS) if 2**power < nb]
    far = [(dist, slot_of[dist]) for dist in dists]
    count = 1 + len(near) + len(far)
    width = count * BLOCK
    scaling = HD ** (-0.5)

    def gathered(buffer, block, sign):
        pieces = [buffer[0, block]]
        for stride in near:
            other = block - sign * stride
            pieces.append(buffer[0, other] if 0 <= other < nb else buffer[1, other % nb])
        for _, slot in far:
            pieces.append(buffer[slot, block])
        return jnp.concatenate(pieces, axis=0)

    lanes = lax.broadcasted_iota(jnp.int32, (1, width), 1)
    levels = lanes // BLOCK
    rows = lax.broadcasted_iota(jnp.int32, (BLOCK, width), 0)
    columns = lax.broadcasted_iota(jnp.int32, (BLOCK, width), 1)
    earlier = columns <= rows
    later = (columns >= rows) | (columns >= BLOCK)

    stat_lane = lax.broadcasted_iota(jnp.int32, (BLOCK, HD), 1)
    stats = jnp.zeros((BLOCK, HD), jnp.float32)
    kept = []
    for block in range(nb):
        keys = gathered(k_all, block, 1)
        values = gathered(v_all, block, 1)
        scores = dot_nt(q_all[0, block], keys) * scaling
        flags = jnp.zeros((1, width), jnp.int32)
        for level in range(count - 1):
            flags = jnp.where(levels == level + 1, kb_ref[block : block + 1, level : level + 1], flags)
        allowed = (flags >= 0) & ((columns >= BLOCK) | earlier)
        scores = jnp.where(allowed, scores, -BIG)
        highest = jnp.max(scores, axis=1, keepdims=True)
        powers = jnp.exp(scores - highest)
        total = jnp.sum(powers, axis=1, keepdims=True)
        probs = powers * (1.0 / total)
        log_total = highest + jnp.log(total)
        attn = dot_nn(probs.astype(jnp.bfloat16), values).astype(jnp.bfloat16)
        a_full[block * BLOCK : (block + 1) * BLOCK, my_columns] = attn
        grads = g_all[0, block]
        inner = jnp.sum(grads.astype(jnp.float32) * attn.astype(jnp.float32), axis=1, keepdims=True)
        stats = jnp.where(stat_lane == block, log_total, stats)
        stats = jnp.where(stat_lane == nb + block, inner, stats)
        kept.append((keys, values, probs, inner))
    turned = jnp.concatenate([stats, stats], axis=0).T[0 : 2 * nb]
    stat_mine[0] = turned
    for level in range(count - 1):
        stat_mine[1 + level, 0:nb] = jnp.where(
            kb_ref[:, level : level + 1] >= 0, turned[0:nb], BIG
        )
        stat_mine[1 + level, nb : 2 * nb] = turned[nb : 2 * nb]
    first_far = 1 + len(near)
    stat_copies = []
    for number, (dist, slot) in enumerate(far):
        low = 1 if dist == 1 else first_far + number
        high = first_far + number + 1
        stat_copies.append(
            pltpu.make_async_remote_copy(
                src_ref=stat_mine.at[low:high],
                dst_ref=stat_got.at[low:high],
                send_sem=stat_send.at[number],
                recv_sem=stat_recv.at[number],
                device_id=seq_peer(-dist),
                device_id_type=MESH,
            )
        )
    for copy in reversed(stat_copies):
        copy.start()
    for copy in a_copies:
        copy.start()

    for block in range(nb):
        keys, values, probs, inner = kept[block]
        grad_probs = dot_nt(g_all[0, block], values)
        grad_scores = (probs * (grad_probs - inner) * scaling).astype(jnp.bfloat16)
        dq_ref[block] = dot_nn(grad_scores, keys).astype(jnp.bfloat16)

    relay(q_copies, most - 1)
    relay(g_copies, most - 1)
    for copy in stat_copies:
        copy.wait_recv()

    half = lax.broadcasted_iota(jnp.int32, (1, 2 * BLOCK), 1) < BLOCK
    for block in range(nb):
        sources = [(stat_mine, 0, block)]
        for number, stride in enumerate(near):
            other = block + stride
            inside = other < nb
            sources.append((stat_mine if inside else stat_got, 1 + number, other % nb))
        for number in range(len(far)):
            sources.append((stat_got, first_far + number, block))

        def stat_row(offset):
            pieces = []
            for index in range(0, count, 2):
                ref, level, row = sources[index]
                piece = ref[level, offset + row : offset + row + 1, :]
                if index + 1 < count:
                    ref, level, row = sources[index + 1]
                    piece = jnp.where(half, piece, ref[level, offset + row : offset + row + 1, :])
                else:
                    piece = piece[:, 0:BLOCK]
                pieces.append(piece)
            return jnp.concatenate(pieces, axis=1)

        askers = gathered(q_all, block, -1)
        grads = gathered(g_all, block, -1)
        scores = dot_nt(k_all[0, block], askers) * scaling
        probs = jnp.exp(jnp.where(later, scores - stat_row(0), -BIG))
        dv_ref[block] = dot_nn(probs.astype(jnp.bfloat16), grads).astype(jnp.bfloat16)
        grad_probs = dot_nt(v_all[0, block], grads)
        grad_scores = (probs * (grad_probs - stat_row(nb)) * scaling).astype(jnp.bfloat16)
        dk_ref[block] = dot_nn(grad_scores, askers).astype(jnp.bfloat16)

    for copy in w_copies:
        copy.wait_recv()
    for copy in a_copies:
        copy.wait_recv()
    mixed_ref[...] = dot_nn(a_full[...], w_col[...]).astype(jnp.bfloat16)

    for copies in (k_copies, v_copies, q_copies, g_copies):
        for dist in dists:
            copies[dist].wait_send()
    for copy in out_copies + w_copies + a_copies + stat_copies:
        copy.wait_send()


def per_device(queries, key_rows, value_rows, key_blocks, out_weight, grad_out):
    n_seq, n_head = lax.axis_size("seq"), lax.axis_size("head")
    rows = queries.shape[0]
    width = out_weight.shape[1]
    nb = rows // BLOCK
    dists = [2**power // nb for power in range(LEVELS) if nb <= 2**power < nb * n_seq]
    blocked = (nb, BLOCK, HD)
    slots = (1 + len(dists),) + blocked
    near = [2**power for power in range(LEVELS) if 2**power < nb]
    count = 1 + len(near) + len(dists)
    vmem = pl.BlockSpec(memory_space=pltpu.VMEM)
    hbm = pl.BlockSpec(memory_space=pl.ANY)
    mixed, dq, dk, dv = pl.pallas_call(
        functools.partial(kernel, n_seq, n_head, dists),
        out_shape=[jax.ShapeDtypeStruct((rows, HD), jnp.bfloat16)]
        + [jax.ShapeDtypeStruct(blocked, jnp.bfloat16)] * 3,
        in_specs=[hbm, hbm, hbm, vmem, hbm, hbm],
        out_specs=[vmem] * 4,
        scratch_shapes=[pltpu.VMEM(slots, jnp.bfloat16)] * 4
        + [
            pltpu.VMEM((rows, width), jnp.bfloat16),
            pltpu.VMEM((HD, width), jnp.bfloat16),
            pltpu.VMEM((width, HD), jnp.bfloat16),
            pltpu.VMEM((rows, width), jnp.bfloat16),
            pltpu.VMEM((count, 2 * nb, HD), jnp.float32),
            pltpu.VMEM((count, 2 * nb, HD), jnp.float32),
            pltpu.SemaphoreType.DMA((4 * len(dists),)),
            pltpu.SemaphoreType.DMA((4 * len(dists),)),
            pltpu.SemaphoreType.DMA((3 * (n_head - 1),)),
            pltpu.SemaphoreType.DMA((3 * (n_head - 1),)),
            pltpu.SemaphoreType.DMA((len(dists),)),
            pltpu.SemaphoreType.DMA((len(dists),)),
            pltpu.SemaphoreType.DMA((6,)),
        ],
        compiler_params=pltpu.CompilerParams(collective_id=0, has_side_effects=True),
    )(
        queries.reshape(blocked),
        key_rows.reshape(blocked),
        value_rows.reshape(blocked),
        key_blocks,
        out_weight,
        grad_out,
    )
    flat = (rows, HD)
    return mixed, dq.reshape(flat), dk.reshape(flat), dv.reshape(flat)


def solution(mesh):
    in_specs = (
        P("seq", "head"),
        P("seq", "head"),
        P("seq", "head"),
        P("seq", None),
        P("head", None),
        P("seq", "head"),
    )
    out_specs = (P("seq", "head"), P("seq", "head"), P("seq", "head"), P("seq", "head"))
    return jax.shard_map(
        per_device, mesh=mesh, in_specs=in_specs, out_specs=out_specs, check_vma=False
    )
```

```python
import functools

import jax
import jax.numpy as jnp
from jax import lax
from jax.experimental import pallas as pl
from jax.experimental.pallas import tpu as pltpu
from jax.sharding import PartitionSpec as P

HD = 128
BLOCK = 64
LEVELS = 9
ROW = 8
MESH = pl.DeviceIdType.MESH
BIG = 1e30


def dot_nt(a, b):
    return lax.dot_general(a, b, (((1,), (1,)), ((), ())), preferred_element_type=jnp.float32)


def dot_nn(a, b):
    return lax.dot_general(a, b, (((1,), (0,)), ((), ())), preferred_element_type=jnp.float32)


class SeqCopies:
    def __init__(self, number, dists, buffer, sign, seq, head, n_seq, send, recv):
        self.buffer, self.sign, self.dists = buffer, sign, dists
        row, col = seq // ROW, lax.rem(seq, ROW)
        self.along = col if sign > 0 else ROW - 1 - col
        self.slot = {dist: 1 + place for place, dist in enumerate(dists)}
        self.extra = 1 + len(dists)
        neighbour = row * ROW + lax.rem(col + (sign + ROW), ROW)
        is_last = self.along // (ROW - 1)
        jump = lambda hop: lax.rem(seq + (sign * hop + n_seq), n_seq)
        base = number * (len(dists) + 1)

        def copy(source, target, place, device):
            return pltpu.make_async_remote_copy(
                src_ref=buffer.at[source],
                dst_ref=buffer.at[target],
                send_sem=send.at[base + place],
                recv_sem=recv.at[base + place],
                device_id=(device, head),
                device_id_type=MESH,
            )

        self.copies = {}
        for place, dist in enumerate(dists):
            slot = self.slot[dist]
            if dist == 1:
                source, device = is_last * self.slot[ROW], neighbour
            elif dist == 2 and dist < ROW:
                one = self.slot[1]
                source, device = one + is_last * (self.extra - one), neighbour
            elif dist == ROW:
                source, device = 0, jump(ROW)
            elif dist == 2 * ROW:
                source, device = self.slot[ROW], jump(ROW)
            else:
                source, device = self.slot[dist // 2], jump(dist // 2)
            self.copies[dist] = copy(source, slot, place, device)
        self.side = copy(self.slot[ROW], self.extra, len(dists), neighbour)

    def start(self):
        self.copies[ROW].start()

        @pl.when(self.along != ROW - 1)
        def _():
            self.copies[1].start()

    def got_row(self):
        self.copies[ROW].wait_recv()
        if 2 * ROW in self.copies:
            self.copies[2 * ROW].start()

        @pl.when(self.along == ROW - 1)
        def _():
            self.copies[1].start()

        @pl.when(self.along == ROW - 2)
        def _():
            self.side.start()

    def got_one(self):
        self.copies[1].wait_recv()

        @pl.when(self.along != ROW - 1)
        def _():
            self.copies[2].start()

        @pl.when(self.along == ROW - 1)
        def _():
            self.side.wait_recv()
            self.copies[2].start()

    def got(self, dist):
        if dist in self.copies:
            self.copies[dist].wait_recv()

    def send(self, dist):
        if dist in self.copies:
            self.copies[dist].start()

    def finish(self):
        for dist in self.dists:
            self.copies[dist].wait_send()

        @pl.when(self.along == ROW - 2)
        def _():
            self.side.wait_send()


class HeadGather:
    def __init__(self, number, own, buffer, seq, head, n_head, send, recv):
        core = lax.rem(head, 2)
        partner = head + 1 - 2 * core
        toward = 2 - 4 * core
        wrap = lambda value: lax.rem(value + 2 * n_head, n_head)

        def columns(who):
            return buffer.at[:, pl.ds(pl.multiple_of(who * HD, HD), HD)]

        def copy(place, who, device, source=None):
            return pltpu.make_async_remote_copy(
                src_ref=columns(who) if source is None else source,
                dst_ref=columns(who),
                send_sem=send.at[7 * number + place],
                recv_sem=recv.at[7 * number + place],
                device_id=(seq, device),
                device_id_type=MESH,
            )

        self.first = [copy(0, head, partner, own)]
        self.relays, self.passes, self.last = [], [], []
        if n_head == 8:
            self.first.append(copy(1, head, wrap(head + toward), own))
            self.first.append(copy(2, head, wrap(head - toward), own))
            self.relays.append(copy(3, wrap(head - toward), wrap(head + toward)))
            self.passes.append(copy(4, wrap(head - toward), partner))
            self.passes.append(copy(5, wrap(head + toward), partner))
            self.last.append(copy(6, wrap(head + 4), partner))

    def start(self):
        for copy in reversed(self.first):
            copy.start()

    def middle(self):
        if self.relays:
            self.first[1].wait_recv()
            self.relays[0].start()
            self.passes[0].start()
            self.first[2].wait_recv()
            self.passes[1].start()

    def late(self):
        if self.relays:
            self.relays[0].wait_recv()
            self.last[0].start()

    def end(self):
        for copy in self.first[:1] + self.passes + self.last:
            copy.wait_recv()

    def finish(self):
        for copy in self.first + self.relays + self.passes + self.last:
            copy.wait_send()


def kernel(
    n_seq, n_head, dists,
    q_hbm, k_hbm, v_hbm, kb_hbm, w_hbm, g_hbm,
    mixed_ref, dq_ref, dk_ref, dv_ref,
    k_all, v_all, q_all, g_all, g_full, w_own, w_col, a_full, stat_mine, stat_got, kb_ref,
    seq_send, seq_recv, head_send, head_recv, w_send, w_recv, stat_send, stat_recv, load_sem,
):
    seq = lax.axis_index("seq")
    head = lax.axis_index("head")
    nb = q_hbm.shape[0]
    my_columns = pl.ds(pl.multiple_of(head * HD, HD), HD)

    load_pairs = [
        (k_hbm, k_all.at[0]),
        (q_hbm, q_all.at[0]),
        (v_hbm, v_all.at[0]),
        (kb_hbm, kb_ref),
        (w_hbm, w_own),
        (g_hbm, g_full.at[:, my_columns]),
        (w_hbm.at[:, my_columns], w_col.at[my_columns, :]),
    ]
    loads = [
        pltpu.make_async_copy(source, target, load_sem.at[place])
        for place, (source, target) in enumerate(load_pairs)
    ]
    for load in loads:
        load.start()

    row, col = seq // ROW, lax.rem(seq, ROW)
    core = lax.rem(head, 2)
    near_seq = [
        row * ROW + lax.rem(col + 1, ROW),
        row * ROW + lax.rem(col + (ROW - 1), ROW),
    ]
    rows_apart = {ROW % n_seq, -ROW % n_seq}
    near_seq += [lax.rem(seq + apart, n_seq) for apart in sorted(rows_apart)]
    near_head = [head + 1 - 2 * core]
    if n_head == 8:
        near_head += [lax.rem(head + 2, n_head), lax.rem(head + (n_head - 2), n_head)]
    barrier = pltpu.get_barrier_semaphore()
    for peer in near_seq:
        pl.semaphore_signal(barrier, inc=1, device_id=(peer, head), device_id_type=MESH)
    for peer in near_head:
        pl.semaphore_signal(barrier, inc=1, device_id=(seq, peer), device_id_type=MESH)
    pl.semaphore_wait(barrier, len(near_seq) + len(near_head))

    where = (seq, head, n_seq, seq_send, seq_recv)
    keys_in = SeqCopies(0, dists, k_all, 1, *where)
    values_in = SeqCopies(1, dists, v_all, 1, *where)
    askers_in = SeqCopies(2, dists, q_all, -1, *where)
    grads_in = SeqCopies(3, dists, g_all, -1, *where)
    out_gather = HeadGather(0, g_hbm, g_full, seq, head, n_head, head_send, head_recv)
    attn_gather = HeadGather(
        1, a_full.at[:, my_columns], a_full, seq, head, n_head, head_send, head_recv
    )
    w_copies = []
    for delta in range(1, n_head):
        peer = lax.rem(head + delta, n_head)
        w_copies.append(
            pltpu.make_async_remote_copy(
                src_ref=w_hbm.at[:, pl.ds(pl.multiple_of(peer * HD, HD), HD)],
                dst_ref=w_col.at[my_columns, :],
                send_sem=w_send.at[delta - 1],
                recv_sem=w_recv.at[delta - 1],
                device_id=(seq, peer),
                device_id_type=MESH,
            )
        )

    out_gather.start()
    loads[0].wait()
    keys_in.start()
    loads[1].wait()
    askers_in.start()
    loads[2].wait()
    values_in.start()

    keys_in.got_row()
    askers_in.got_row()
    out_gather.middle()
    keys_in.got_one()
    askers_in.got_one()
    values_in.got_row()
    values_in.got_one()
    out_gather.late()
    for load in loads[3:]:
        load.wait()
    out_gather.end()
    for copy in w_copies:
        copy.start()
    g_own = dot_nt(g_full[...], w_own[...]).astype(jnp.bfloat16)
    for block in range(nb):
        g_all[0, block] = g_own[block * BLOCK : (block + 1) * BLOCK]
    grads_in.start()
    for dist in (2, 2 * ROW):
        keys_in.got(dist)
        askers_in.got(dist)
    for dist in (2, 2 * ROW):
        if dist * 2 != ROW:
            keys_in.send(dist * 2)
            askers_in.send(dist * 2)
    for dist in (2, 2 * ROW):
        values_in.got(dist)
        if dist * 2 != ROW:
            values_in.send(dist * 2)
    grads_in.got_row()
    grads_in.got_one()
    for dist in (4, 4 * ROW):
        if dist != ROW:
            keys_in.got(dist)

    near = [2**power for power in range(LEVELS) if 2**power < nb]
    far = [(dist, 1 + place) for place, dist in enumerate(dists)]
    count = 1 + len(near) + len(far)
    width = count * BLOCK
    scaling = HD ** (-0.5)

    def gathered(buffer, block, sign):
        pieces = [buffer[0, block]]
        for stride in near:
            other = block - sign * stride
            pieces.append(buffer[0, other] if 0 <= other < nb else buffer[1, other % nb])
        for _, slot in far:
            pieces.append(buffer[slot, block])
        return jnp.concatenate(pieces, axis=0)

    lanes = lax.broadcasted_iota(jnp.int32, (1, width), 1)
    levels = lanes // BLOCK
    rows = lax.broadcasted_iota(jnp.int32, (BLOCK, width), 0)
    columns = lax.broadcasted_iota(jnp.int32, (BLOCK, width), 1)
    earlier = columns <= rows
    later = (columns >= rows) | (columns >= BLOCK)

    kept = []
    for block in range(nb):
        scores = dot_nt(q_all[0, block], gathered(k_all, block, 1)) * scaling
        flags = jnp.zeros((1, width), jnp.int32)
        for level in range(count - 1):
            flags = jnp.where(levels == level + 1, kb_ref[block : block + 1, level : level + 1], flags)
        allowed = (flags >= 0) & ((columns >= BLOCK) | earlier)
        scores = jnp.where(allowed, scores, -BIG)
        highest = jnp.max(scores, axis=1, keepdims=True)
        powers = jnp.exp(scores - highest)
        total = jnp.sum(powers, axis=1, keepdims=True)
        probs = powers * (1.0 / total)
        log_total = highest + jnp.log(total)
        kept.append((probs, log_total))

    for dist in (2, 2 * ROW):
        grads_in.got(dist)
        if dist * 2 != ROW:
            grads_in.send(dist * 2)
    for dist in (4, 4 * ROW):
        if dist != ROW:
            values_in.got(dist)

    stat_lane = lax.broadcasted_iota(jnp.int32, (BLOCK, HD), 1)
    stats = jnp.zeros((BLOCK, HD), jnp.float32)
    inners = []
    for block in range(nb):
        probs, log_total = kept[block]
        attn = dot_nn(probs.astype(jnp.bfloat16), gathered(v_all, block, 1)).astype(jnp.bfloat16)
        a_full[block * BLOCK : (block + 1) * BLOCK, my_columns] = attn
        grads = g_all[0, block]
        inner = jnp.sum(grads.astype(jnp.float32) * attn.astype(jnp.float32), axis=1, keepdims=True)
        stats = jnp.where(stat_lane == block, log_total, stats)
        stats = jnp.where(stat_lane == nb + block, inner, stats)
        inners.append(inner)
    turned = jnp.concatenate([stats, stats], axis=0).T[0 : 2 * nb]
    stat_mine[0] = turned
    for level in range(count - 1):
        stat_mine[1 + level, 0:nb] = jnp.where(
            kb_ref[:, level : level + 1] >= 0, turned[0:nb], BIG
        )
        stat_mine[1 + level, nb : 2 * nb] = turned[nb : 2 * nb]
    first_far = 1 + len(near)
    stat_copies = []
    for number, (dist, slot) in enumerate(far):
        low = 1 if dist == 1 else first_far + number
        high = first_far + number + 1
        stat_copies.append(
            pltpu.make_async_remote_copy(
                src_ref=stat_mine.at[low:high],
                dst_ref=stat_got.at[low:high],
                send_sem=stat_send.at[number],
                recv_sem=stat_recv.at[number],
                device_id=(lax.rem(seq + (n_seq - dist), n_seq), head),
                device_id_type=MESH,
            )
        )
    for copy in reversed(stat_copies):
        copy.start()
    attn_gather.start()

    for block in range(nb):
        probs, _ = kept[block]
        grad_probs = dot_nt(g_all[0, block], gathered(v_all, block, 1))
        grad_scores = (probs * (grad_probs - inners[block]) * scaling).astype(jnp.bfloat16)
        dq_ref[block] = dot_nn(grad_scores, gathered(k_all, block, 1)).astype(jnp.bfloat16)
        if block == nb // 2:
            attn_gather.middle()

    for dist in (4, 4 * ROW):
        if dist != ROW:
            askers_in.got(dist)
            grads_in.got(dist)
    attn_gather.late()
    for copy in stat_copies:
        copy.wait_recv()

    half = lax.broadcasted_iota(jnp.int32, (1, 2 * BLOCK), 1) < BLOCK
    for block in range(nb):
        sources = [(stat_mine, 0, block)]
        for number, stride in enumerate(near):
            other = block + stride
            inside = other < nb
            sources.append((stat_mine if inside else stat_got, 1 + number, other % nb))
        for number in range(len(far)):
            sources.append((stat_got, first_far + number, block))

        def stat_row(offset):
            pieces = []
            for index in range(0, count, 2):
                ref, level, line = sources[index]
                piece = ref[level, offset + line : offset + line + 1, :]
                if index + 1 < count:
                    ref, level, line = sources[index + 1]
                    piece = jnp.where(half, piece, ref[level, offset + line : offset + line + 1, :])
                else:
                    piece = piece[:, 0:BLOCK]
                pieces.append(piece)
            return jnp.concatenate(pieces, axis=1)

        askers = gathered(q_all, block, -1)
        grads = gathered(g_all, block, -1)
        scores = dot_nt(k_all[0, block], askers) * scaling
        probs = jnp.exp(jnp.where(later, scores - stat_row(0), -BIG))
        dv_ref[block] = dot_nn(probs.astype(jnp.bfloat16), grads).astype(jnp.bfloat16)
        grad_probs = dot_nt(v_all[0, block], grads)
        grad_scores = (probs * (grad_probs - stat_row(nb)) * scaling).astype(jnp.bfloat16)
        dk_ref[block] = dot_nn(grad_scores, askers).astype(jnp.bfloat16)

    for copy in w_copies:
        copy.wait_recv()
    attn_gather.end()
    mixed_ref[...] = dot_nn(a_full[...], w_col[...]).astype(jnp.bfloat16)

    for part in (keys_in, values_in, askers_in, grads_in, out_gather, attn_gather):
        part.finish()
    for copy in w_copies + stat_copies:
        copy.wait_send()


def put_out(*refs):
    count = len(refs) // 2
    for source, target in zip(refs[:count], refs[count:]):
        target[...] = source[...]


def per_device(queries, key_rows, value_rows, key_blocks, out_weight, grad_out):
    n_seq, n_head = lax.axis_size("seq"), lax.axis_size("head")
    rows = queries.shape[0]
    width = out_weight.shape[1]
    nb = rows // BLOCK
    dists = [2**power // nb for power in range(LEVELS) if nb <= 2**power < nb * n_seq]
    blocked = (nb, BLOCK, HD)
    slots = (2 + len(dists),) + blocked
    near = [2**power for power in range(LEVELS) if 2**power < nb]
    count = 1 + len(near) + len(dists)
    vmem = pl.BlockSpec(memory_space=pltpu.VMEM)
    hbm = pl.BlockSpec(memory_space=pltpu.HBM)
    seq_sems = pltpu.SemaphoreType.DMA((4 * (len(dists) + 1),))
    results = pl.pallas_call(
        functools.partial(kernel, n_seq, n_head, dists),
        out_shape=[jax.ShapeDtypeStruct((rows, HD), jnp.bfloat16)]
        + [jax.ShapeDtypeStruct(blocked, jnp.bfloat16)] * 3,
        in_specs=[hbm] * 6,
        out_specs=[vmem] * 4,
        scratch_shapes=[pltpu.VMEM(slots, jnp.bfloat16)] * 4
        + [
            pltpu.VMEM((rows, width), jnp.bfloat16),
            pltpu.VMEM((HD, width), jnp.bfloat16),
            pltpu.VMEM((width, HD), jnp.bfloat16),
            pltpu.VMEM((rows, width), jnp.bfloat16),
            pltpu.VMEM((count, 2 * nb, HD), jnp.float32),
            pltpu.VMEM((count, 2 * nb, HD), jnp.float32),
            pltpu.VMEM(key_blocks.shape, jnp.int32),
            seq_sems,
            seq_sems,
            pltpu.SemaphoreType.DMA((14,)),
            pltpu.SemaphoreType.DMA((14,)),
            pltpu.SemaphoreType.DMA((n_head - 1,)),
            pltpu.SemaphoreType.DMA((n_head - 1,)),
            pltpu.SemaphoreType.DMA((len(dists),)),
            pltpu.SemaphoreType.DMA((len(dists),)),
            pltpu.SemaphoreType.DMA((7,)),
        ],
        compiler_params=pltpu.CompilerParams(
            collective_id=0, has_side_effects=True, vmem_limit_bytes=20 * 2**20
        ),
        name="attention",
    )(
        *[
            pltpu.with_memory_space_constraint(array, pltpu.HBM)
            for array in (
                queries.reshape(blocked),
                key_rows.reshape(blocked),
                value_rows.reshape(blocked),
                key_blocks,
                out_weight,
                grad_out,
            )
        ]
    )
    results = pl.pallas_call(
        put_out,
        out_shape=[jax.ShapeDtypeStruct(result.shape, result.dtype) for result in results],
        in_specs=[vmem] * 4,
        out_specs=[vmem] * 4,
        compiler_params=pltpu.CompilerParams(vmem_limit_bytes=8 * 2**20),
        name="put_out",
    )(*results)
    return tuple(result.reshape(rows, HD) for result in results)


def solution(mesh):
    in_specs = (
        P("seq", "head"),
        P("seq", "head"),
        P("seq", "head"),
        P("seq", None),
        P("head", None),
        P("seq", "head"),
    )
    out_specs = (P("seq", "head"), P("seq", "head"), P("seq", "head"), P("seq", "head"))
    return jax.shard_map(
        per_device, mesh=mesh, in_specs=in_specs, out_specs=out_specs, check_vma=False
    )
```

```python
import functools

import jax
import jax.numpy as jnp
from jax import lax
from jax.experimental import pallas as pl
from jax.experimental.pallas import tpu as pltpu
from jax.sharding import PartitionSpec as P

HD = 128
BLOCK = 64
LEVELS = 9
ROW = 8
MESH = pl.DeviceIdType.MESH
BIG = 1e30


def dot_nt(a, b):
    return lax.dot_general(a, b, (((1,), (1,)), ((), ())), preferred_element_type=jnp.float32)


def dot_nn(a, b):
    return lax.dot_general(a, b, (((1,), (0,)), ((), ())), preferred_element_type=jnp.float32)


class SeqCopies:
    def __init__(self, number, dists, buffer, sign, seq, head, n_seq, send, recv):
        self.dists, self.ahead = dists, sign > 0
        row, self.col = seq // ROW, lax.rem(seq, ROW)
        along = self.col if sign > 0 else ROW - 1 - self.col
        self.side_col = ROW - 2 if sign > 0 else 1
        self.slot = {dist: 1 + place for place, dist in enumerate(dists)}
        self.extra = 1 + len(dists)
        neighbour = row * ROW + lax.rem(self.col + (sign + ROW), ROW)
        is_last = along // (ROW - 1)
        jump = lambda hop: lax.rem(seq + (sign * hop + n_seq), n_seq)
        base = number * (len(dists) + 1)

        def copy(source, target, place, device):
            return pltpu.make_async_remote_copy(
                src_ref=buffer.at[source],
                dst_ref=buffer.at[target],
                send_sem=send.at[base + place],
                recv_sem=recv.at[base + place],
                device_id=(device, head),
                device_id_type=MESH,
            )

        self.copies = {}
        for place, dist in enumerate(dists):
            slot = self.slot[dist]
            if dist == 1:
                source, device = is_last * self.slot[ROW], neighbour
            elif dist == 2 and dist < ROW:
                one = self.slot[1]
                source, device = one + is_last * (self.extra - one), neighbour
            elif dist == ROW:
                source, device = 0, jump(ROW)
            elif dist == 2 * ROW:
                source, device = self.slot[ROW], jump(ROW)
            else:
                source, device = self.slot[dist // 2], jump(dist // 2)
            self.copies[dist] = copy(source, slot, place, device)
        self.side = copy(self.slot[ROW], self.extra, len(dists), neighbour)

    def when(self, low, high, *steps):
        @pl.when((self.col >= low) & (self.col <= high))
        def _():
            self.do(*steps)

    def do(self, *steps):
        for step, dist in steps:
            if dist in self.copies or dist == 0:
                copy = self.copies[dist] if dist else self.side
                copy.wait_recv() if step == "w" else copy.start()

    def start(self):
        self.do(("s", ROW))
        if self.ahead:
            self.when(0, ROW - 2, ("s", 1))
        else:
            self.when(1, ROW - 1, ("s", 1))

    def got_row(self):
        self.do(("w", ROW), ("s", 2 * ROW))
        self.when(self.side_col, self.side_col, ("s", 0))
        if self.ahead:
            self.when(ROW - 1, ROW - 1, ("s", 1))

    def got_far(self):
        self.do(("w", 2 * ROW), ("s", 4 * ROW))

    def finish(self):
        for dist in self.dists:
            self.copies[dist].wait_send()

        @pl.when(self.col == self.side_col)
        def _():
            self.side.wait_send()


class HeadGather:
    def __init__(self, number, own, buffer, seq, head, n_head, send, recv):
        core = lax.rem(head, 2)
        partner = head + 1 - 2 * core
        toward = 2 - 4 * core
        wrap = lambda value: lax.rem(value + 2 * n_head, n_head)

        def columns(who):
            return buffer.at[:, pl.ds(pl.multiple_of(who * HD, HD), HD)]

        def copy(place, who, device, source=None):
            return pltpu.make_async_remote_copy(
                src_ref=columns(who) if source is None else source,
                dst_ref=columns(who),
                send_sem=send.at[7 * number + place],
                recv_sem=recv.at[7 * number + place],
                device_id=(seq, device),
                device_id_type=MESH,
            )

        self.first = [copy(0, head, partner, own)]
        self.relays, self.passes, self.last = [], [], []
        if n_head == 8:
            self.first.append(copy(1, head, wrap(head + toward), own))
            self.first.append(copy(2, head, wrap(head - toward), own))
            self.relays.append(copy(3, wrap(head - toward), wrap(head + toward)))
            self.passes.append(copy(4, wrap(head - toward), partner))
            self.passes.append(copy(5, wrap(head + toward), partner))
            self.last.append(copy(6, wrap(head + 4), partner))

    def start(self):
        for copy in reversed(self.first):
            copy.start()

    def middle(self):
        if self.relays:
            self.first[1].wait_recv()
            self.relays[0].start()
            self.passes[0].start()
            self.first[2].wait_recv()
            self.passes[1].start()

    def late(self):
        if self.relays:
            self.relays[0].wait_recv()
            self.last[0].start()

    def end(self):
        for copy in self.first[:1] + self.passes + self.last:
            copy.wait_recv()

    def finish(self):
        for copy in self.first + self.relays + self.passes + self.last:
            copy.wait_send()


def kernel(
    n_seq, n_head, dists,
    q_hbm, k_hbm, v_hbm, kb_hbm, w_hbm, g_hbm,
    mixed_ref, dq_ref, dk_ref, dv_ref,
    k_all, v_all, q_all, g_all, g_full, w_own, w_col, a_full, stat_mine, stat_got, kb_ref,
    seq_send, seq_recv, head_send, head_recv, w_send, w_recv, stat_send, stat_recv, load_sem, wrap_sem,
):
    seq = lax.axis_index("seq")
    head = lax.axis_index("head")
    nb = q_hbm.shape[0]
    my_columns = pl.ds(pl.multiple_of(head * HD, HD), HD)

    load_pairs = [
        (k_hbm, k_all.at[0]),
        (q_hbm, q_all.at[0]),
        (v_hbm, v_all.at[0]),
        (kb_hbm, kb_ref),
        (w_hbm, w_own),
        (g_hbm, g_full.at[:, my_columns]),
        (w_hbm.at[:, my_columns], w_col.at[my_columns, :]),
    ]
    loads = [
        pltpu.make_async_copy(source, target, load_sem.at[place])
        for place, (source, target) in enumerate(load_pairs)
    ]
    for load in loads:
        load.start()

    row, col = seq // ROW, lax.rem(seq, ROW)
    core = lax.rem(head, 2)
    last = ROW - 1
    in_row = [dist for dist in dists if dist < ROW]
    four = 4 in in_row
    barrier = pltpu.get_barrier_semaphore()

    def greet(peer_seq, peer_head, semaphore=barrier):
        pl.semaphore_signal(
            semaphore, inc=1, device_id=(peer_seq, peer_head), device_id_type=MESH
        )

    @pl.when(col < last)
    def _():
        greet(seq + 1, head)

    @pl.when(col > 0)
    def _():
        greet(seq - 1, head)

    @pl.when(col == 0)
    def _():
        greet(seq + last, head)

    if four:

        @pl.when(col < 2)
        def _():
            greet(lax.rem(seq + (n_seq - 2), n_seq), head)

    rows_apart = sorted({ROW % n_seq, -ROW % n_seq})
    near_head = [head + 1 - 2 * core]
    if n_head == 8:
        near_head += [lax.rem(head + 2, n_head), lax.rem(head + (n_head - 2), n_head)]
    for apart in rows_apart:
        greet(lax.rem(seq + apart, n_seq), head)
    for peer in near_head:
        greet(seq, peer)
    expected = len(rows_apart) + len(near_head) + 2 - (last - col) // last
    if four:
        expected = expected + col // (last - 1)
    pl.semaphore_wait(barrier, expected)

    @pl.when(col == last)
    def _():
        greet(seq - last, head, wrap_sem)

    where = (seq, head, n_seq, seq_send, seq_recv)
    keys_in = SeqCopies(0, dists, k_all, 1, *where)
    values_in = SeqCopies(1, dists, v_all, 1, *where)
    askers_in = SeqCopies(2, dists, q_all, -1, *where)
    grads_in = SeqCopies(3, dists, g_all, -1, *where)
    out_gather = HeadGather(0, g_hbm, g_full, seq, head, n_head, head_send, head_recv)
    attn_gather = HeadGather(
        1, a_full.at[:, my_columns], a_full, seq, head, n_head, head_send, head_recv
    )
    w_copies = []
    for delta in range(1, n_head):
        peer = lax.rem(head + delta, n_head)
        w_copies.append(
            pltpu.make_async_remote_copy(
                src_ref=w_hbm.at[:, pl.ds(pl.multiple_of(peer * HD, HD), HD)],
                dst_ref=w_col.at[my_columns, :],
                send_sem=w_send.at[delta - 1],
                recv_sem=w_recv.at[delta - 1],
                device_id=(seq, peer),
                device_id_type=MESH,
            )
        )

    out_gather.start()
    loads[0].wait()
    keys_in.start()
    loads[1].wait()
    askers_in.start()
    loads[2].wait()
    values_in.start()

    keys_in.got_row()
    askers_in.got_row()
    out_gather.middle()
    keys_in.when(1, last - 1, ("w", 1), ("s", 2))
    keys_in.when(last, last, ("w", 1), ("w", 0), ("s", 2))
    askers_in.when(0, 0, ("w", 1))
    askers_in.when(1, last - 1, ("w", 1), ("s", 2))
    values_in.got_row()
    values_in.when(1, last - 1, ("w", 1), ("s", 2))
    values_in.when(last, last, ("w", 1), ("w", 0), ("s", 2))
    out_gather.late()
    for load in loads[3:]:
        load.wait()
    out_gather.end()
    for copy in w_copies:
        copy.start()
    g_own = dot_nt(g_full[...], w_own[...]).astype(jnp.bfloat16)
    for block in range(nb):
        g_all[0, block] = g_own[block * BLOCK : (block + 1) * BLOCK]
    grads_in.start()
    two, then = ("w", 2), [("s", 4)] if four else []
    keys_in.do(("w", 2 * ROW))
    askers_in.do(("w", 2 * ROW))
    keys_in.do(("s", 4 * ROW))
    askers_in.do(("s", 4 * ROW))
    keys_in.when(2, last, two)
    askers_in.when(0, last - 2, two)
    keys_in.when(2, last, *then)
    askers_in.when(2, last - 2, *then)
    values_in.got_far()
    values_in.when(2, last, two, *then)
    grads_in.got_row()
    askers_in.when(last, last, ("w", 1), ("s", 2))

    @pl.when(col == 0)
    def _():
        pl.semaphore_wait(wrap_sem, 1)
        askers_in.do(("s", 1), ("w", 0), ("s", 2))

    grads_in.when(0, 0, ("w", 1), ("s", 1), ("w", 0), ("s", 2))
    grads_in.when(1, last - 1, ("w", 1), ("s", 2))
    askers_in.when(last - 1, last, two, *then)
    grads_in.when(last, last, ("w", 1), ("s", 2))
    grads_in.got_far()
    grads_in.do(two)
    grads_in.when(2, last, *then)
    keys_in.when(0, 0, ("w", 1), ("s", 2))
    values_in.when(0, 0, ("w", 1), ("s", 2))
    keys_in.when(0, 1, two, *then)
    askers_in.when(0, 1, *then)
    values_in.when(0, 1, two, *then)
    grads_in.when(0, 1, *then)
    keys_in.do(("w", 4 * ROW))
    if four:
        keys_in.do(("w", 4))

    near = [2**power for power in range(LEVELS) if 2**power < nb]
    far = [(dist, 1 + place) for place, dist in enumerate(dists)]
    count = 1 + len(near) + len(far)
    width = count * BLOCK
    scaling = HD ** (-0.5)

    def gathered(buffer, block, sign):
        pieces = [buffer[0, block]]
        for stride in near:
            other = block - sign * stride
            pieces.append(buffer[0, other] if 0 <= other < nb else buffer[1, other % nb])
        for _, slot in far:
            pieces.append(buffer[slot, block])
        return jnp.concatenate(pieces, axis=0)

    lanes = lax.broadcasted_iota(jnp.int32, (1, width), 1)
    levels = lanes // BLOCK
    rows = lax.broadcasted_iota(jnp.int32, (BLOCK, width), 0)
    columns = lax.broadcasted_iota(jnp.int32, (BLOCK, width), 1)
    earlier = columns <= rows
    later = (columns >= rows) | (columns >= BLOCK)

    kept = []
    for block in range(nb):
        scores = dot_nt(q_all[0, block], gathered(k_all, block, 1)) * scaling
        flags = jnp.zeros((1, width), jnp.int32)
        for level in range(count - 1):
            flags = jnp.where(levels == level + 1, kb_ref[block : block + 1, level : level + 1], flags)
        allowed = (flags >= 0) & ((columns >= BLOCK) | earlier)
        scores = jnp.where(allowed, scores, -BIG)
        highest = jnp.max(scores, axis=1, keepdims=True)
        powers = jnp.exp(scores - highest)
        total = jnp.sum(powers, axis=1, keepdims=True)
        probs = powers * (1.0 / total)
        log_total = highest + jnp.log(total)
        kept.append((probs, log_total))

    values_in.do(("w", 4 * ROW))
    if four:
        values_in.do(("w", 4))

    stat_lane = lax.broadcasted_iota(jnp.int32, (BLOCK, HD), 1)
    stats = jnp.zeros((BLOCK, HD), jnp.float32)
    inners = []
    for block in range(nb):
        probs, log_total = kept[block]
        attn = dot_nn(probs.astype(jnp.bfloat16), gathered(v_all, block, 1)).astype(jnp.bfloat16)
        a_full[block * BLOCK : (block + 1) * BLOCK, my_columns] = attn
        grads = g_all[0, block]
        inner = jnp.sum(grads.astype(jnp.float32) * attn.astype(jnp.float32), axis=1, keepdims=True)
        stats = jnp.where(stat_lane == block, log_total, stats)
        stats = jnp.where(stat_lane == nb + block, inner, stats)
        inners.append(inner)
    turned = jnp.concatenate([stats, stats], axis=0).T[0 : 2 * nb]
    stat_mine[0] = turned
    for level in range(count - 1):
        stat_mine[1 + level, 0:nb] = jnp.where(
            kb_ref[:, level : level + 1] >= 0, turned[0:nb], BIG
        )
        stat_mine[1 + level, nb : 2 * nb] = turned[nb : 2 * nb]
    first_far = 1 + len(near)
    stat_copies = []
    for number, (dist, slot) in enumerate(far):
        low = 1 if dist == 1 else first_far + number
        high = first_far + number + 1
        stat_copies.append(
            pltpu.make_async_remote_copy(
                src_ref=stat_mine.at[low:high],
                dst_ref=stat_got.at[low:high],
                send_sem=stat_send.at[number],
                recv_sem=stat_recv.at[number],
                device_id=(lax.rem(seq + (n_seq - dist), n_seq), head),
                device_id_type=MESH,
            )
        )
    for copy in reversed(stat_copies):
        copy.start()
    attn_gather.start()

    for block in range(nb):
        probs, _ = kept[block]
        grad_probs = dot_nt(g_all[0, block], gathered(v_all, block, 1))
        grad_scores = (probs * (grad_probs - inners[block]) * scaling).astype(jnp.bfloat16)
        dq_ref[block] = dot_nn(grad_scores, gathered(k_all, block, 1)).astype(jnp.bfloat16)
        if block == nb // 2:
            attn_gather.middle()

    for tensor in (askers_in, grads_in):
        tensor.do(("w", 4 * ROW))
        if four:
            tensor.do(("w", 4))
    attn_gather.late()
    for copy in stat_copies:
        copy.wait_recv()

    half = lax.broadcasted_iota(jnp.int32, (1, 2 * BLOCK), 1) < BLOCK
    for block in range(nb):
        sources = [(stat_mine, 0, block)]
        for number, stride in enumerate(near):
            other = block + stride
            inside = other < nb
            sources.append((stat_mine if inside else stat_got, 1 + number, other % nb))
        for number in range(len(far)):
            sources.append((stat_got, first_far + number, block))

        def stat_row(offset):
            pieces = []
            for index in range(0, count, 2):
                ref, level, line = sources[index]
                piece = ref[level, offset + line : offset + line + 1, :]
                if index + 1 < count:
                    ref, level, line = sources[index + 1]
                    piece = jnp.where(half, piece, ref[level, offset + line : offset + line + 1, :])
                else:
                    piece = piece[:, 0:BLOCK]
                pieces.append(piece)
            return jnp.concatenate(pieces, axis=1)

        askers = gathered(q_all, block, -1)
        grads = gathered(g_all, block, -1)
        scores = dot_nt(k_all[0, block], askers) * scaling
        probs = jnp.exp(jnp.where(later, scores - stat_row(0), -BIG))
        dv_ref[block] = dot_nn(probs.astype(jnp.bfloat16), grads).astype(jnp.bfloat16)
        grad_probs = dot_nt(v_all[0, block], grads)
        grad_scores = (probs * (grad_probs - stat_row(nb)) * scaling).astype(jnp.bfloat16)
        dk_ref[block] = dot_nn(grad_scores, askers).astype(jnp.bfloat16)

    for copy in w_copies:
        copy.wait_recv()
    attn_gather.end()
    mixed_ref[...] = dot_nn(a_full[...], w_col[...]).astype(jnp.bfloat16)

    for part in (keys_in, values_in, askers_in, grads_in, out_gather, attn_gather):
        part.finish()
    for copy in w_copies + stat_copies:
        copy.wait_send()


def put_out(*refs):
    count = len(refs) // 2
    for source, target in zip(refs[:count], refs[count:]):
        target[...] = source[...]


def per_device(queries, key_rows, value_rows, key_blocks, out_weight, grad_out):
    n_seq, n_head = lax.axis_size("seq"), lax.axis_size("head")
    rows = queries.shape[0]
    width = out_weight.shape[1]
    nb = rows // BLOCK
    dists = [2**power // nb for power in range(LEVELS) if nb <= 2**power < nb * n_seq]
    blocked = (nb, BLOCK, HD)
    slots = (2 + len(dists),) + blocked
    near = [2**power for power in range(LEVELS) if 2**power < nb]
    count = 1 + len(near) + len(dists)
    vmem = pl.BlockSpec(memory_space=pltpu.VMEM)
    hbm = pl.BlockSpec(memory_space=pltpu.HBM)
    seq_sems = pltpu.SemaphoreType.DMA((4 * (len(dists) + 1),))
    results = pl.pallas_call(
        functools.partial(kernel, n_seq, n_head, dists),
        out_shape=[jax.ShapeDtypeStruct((rows, HD), jnp.bfloat16)]
        + [jax.ShapeDtypeStruct(blocked, jnp.bfloat16)] * 3,
        in_specs=[hbm] * 6,
        out_specs=[vmem] * 4,
        scratch_shapes=[pltpu.VMEM(slots, jnp.bfloat16)] * 4
        + [
            pltpu.VMEM((rows, width), jnp.bfloat16),
            pltpu.VMEM((HD, width), jnp.bfloat16),
            pltpu.VMEM((width, HD), jnp.bfloat16),
            pltpu.VMEM((rows, width), jnp.bfloat16),
            pltpu.VMEM((count, 2 * nb, HD), jnp.float32),
            pltpu.VMEM((count, 2 * nb, HD), jnp.float32),
            pltpu.VMEM(key_blocks.shape, jnp.int32),
            seq_sems,
            seq_sems,
            pltpu.SemaphoreType.DMA((14,)),
            pltpu.SemaphoreType.DMA((14,)),
            pltpu.SemaphoreType.DMA((n_head - 1,)),
            pltpu.SemaphoreType.DMA((n_head - 1,)),
            pltpu.SemaphoreType.DMA((len(dists),)),
            pltpu.SemaphoreType.DMA((len(dists),)),
            pltpu.SemaphoreType.DMA((7,)),
            pltpu.SemaphoreType.REGULAR,
        ],
        compiler_params=pltpu.CompilerParams(
            collective_id=0, has_side_effects=True, vmem_limit_bytes=20 * 2**20
        ),
        name="attention",
    )(
        *[
            pltpu.with_memory_space_constraint(array, pltpu.HBM)
            for array in (
                queries.reshape(blocked),
                key_rows.reshape(blocked),
                value_rows.reshape(blocked),
                key_blocks,
                out_weight,
                grad_out,
            )
        ]
    )
    results = pl.pallas_call(
        put_out,
        out_shape=[jax.ShapeDtypeStruct(result.shape, result.dtype) for result in results],
        in_specs=[vmem] * 4,
        out_specs=[vmem] * 4,
        compiler_params=pltpu.CompilerParams(vmem_limit_bytes=8 * 2**20),
        name="put_out",
    )(*results)
    return tuple(result.reshape(rows, HD) for result in results)


def solution(mesh):
    in_specs = (
        P("seq", "head"),
        P("seq", "head"),
        P("seq", "head"),
        P("seq", None),
        P("head", None),
        P("seq", "head"),
    )
    out_specs = (P("seq", "head"), P("seq", "head"), P("seq", "head"), P("seq", "head"))
    return jax.shard_map(
        per_device, mesh=mesh, in_specs=in_specs, out_specs=out_specs, check_vma=False
    )
```

```python
import functools

import jax
import jax.numpy as jnp
from jax import lax
from jax.experimental import pallas as pl
from jax.experimental.pallas import tpu as pltpu
from jax.sharding import PartitionSpec as P

HD = 128
BLOCK = 64
LEVELS = 9
ROW = 8
MESH = pl.DeviceIdType.MESH
BIG = 1e30


def dot_nt(a, b):
    return lax.dot_general(a, b, (((1,), (1,)), ((), ())), preferred_element_type=jnp.float32)


def dot_nn(a, b):
    return lax.dot_general(a, b, (((1,), (0,)), ((), ())), preferred_element_type=jnp.float32)


class SeqCopies:
    def __init__(self, number, dists, buffer, sign, seq, head, n_seq, send, recv, straight=False):
        self.dists, self.ahead = dists, sign > 0
        row, self.col = seq // ROW, lax.rem(seq, ROW)
        along = self.col if sign > 0 else ROW - 1 - self.col
        self.slot = {dist: 1 + place for place, dist in enumerate(dists)}
        in_row = lambda hop: row * ROW + lax.rem(self.col + (sign * hop + ROW), ROW)
        jump = lambda hop: lax.rem(seq + (sign * hop + n_seq), n_seq)
        base = number * len(dists)

        def copy(source, target, place, device):
            return pltpu.make_async_remote_copy(
                src_ref=buffer.at[source],
                dst_ref=buffer.at[target],
                send_sem=send.at[base + place],
                recv_sem=recv.at[base + place],
                device_id=(device, head),
                device_id_type=MESH,
            )

        self.copies = {}
        for place, dist in enumerate(dists):
            slot = self.slot[dist]
            if dist <= 2:
                source, device = along // (ROW - dist) * self.slot[ROW], in_row(dist)
            elif dist == ROW:
                source, device = 0, jump(ROW)
            elif dist == 2 * ROW and straight:
                source, device = 0, jump(2 * ROW)
            elif dist == 2 * ROW:
                source, device = self.slot[ROW], jump(ROW)
            else:
                source, device = self.slot[dist // 2], jump(dist // 2)
            self.copies[dist] = copy(source, slot, place, device)

    def when(self, low, high, *steps):
        @pl.when((self.col >= low) & (self.col <= high))
        def _():
            self.do(*steps)

    def do(self, *steps):
        for step, dist in steps:
            if dist in self.copies:
                copy = self.copies[dist]
                copy.wait_recv() if step == "w" else copy.start()

    def finish(self):
        for dist in self.dists:
            self.copies[dist].wait_send()


class HeadGather:
    def __init__(self, number, own, buffer, seq, head, n_head, send, recv):
        core = lax.rem(head, 2)
        partner = head + 1 - 2 * core
        toward = 2 - 4 * core
        wrap = lambda value: lax.rem(value + 2 * n_head, n_head)

        def columns(who):
            return buffer.at[:, pl.ds(pl.multiple_of(who * HD, HD), HD)]

        def copy(place, who, device, source=None):
            return pltpu.make_async_remote_copy(
                src_ref=columns(who) if source is None else source,
                dst_ref=columns(who),
                send_sem=send.at[7 * number + place],
                recv_sem=recv.at[7 * number + place],
                device_id=(seq, device),
                device_id_type=MESH,
            )

        self.first = [copy(0, head, partner, own)]
        self.relays, self.passes, self.last = [], [], []
        if n_head == 8:
            self.first.append(copy(1, head, wrap(head + toward), own))
            self.first.append(copy(2, head, wrap(head - toward), own))
            self.relays.append(copy(3, wrap(head - toward), wrap(head + toward)))
            self.passes.append(copy(4, wrap(head - toward), partner))
            self.passes.append(copy(5, wrap(head + toward), partner))
            self.last.append(copy(6, wrap(head + 4), partner))

    def start(self):
        for copy in reversed(self.first):
            copy.start()

    def middle(self):
        if self.relays:
            self.first[1].wait_recv()
            self.relays[0].start()
            self.passes[0].start()
            self.first[2].wait_recv()
            self.passes[1].start()

    def late(self):
        if self.relays:
            self.relays[0].wait_recv()
            self.last[0].start()

    def end(self):
        for copy in self.first[:1] + self.passes + self.last:
            copy.wait_recv()

    def finish(self):
        for copy in self.first + self.relays + self.passes + self.last:
            copy.wait_send()


def kernel(
    n_seq, n_head, dists,
    q_hbm, k_hbm, v_hbm, kb_hbm, w_hbm, g_hbm,
    mixed_ref, dq_ref, dk_ref, dv_ref,
    k_all, v_all, q_all, g_all, g_full, w_own, w_col, a_full, stat_mine, stat_got, kb_ref,
    seq_send, seq_recv, head_send, head_recv, w_send, w_recv, stat_send, stat_recv, load_sem, ready_sems,
):
    seq = lax.axis_index("seq")
    head = lax.axis_index("head")
    nb = q_hbm.shape[0]
    my_columns = pl.ds(pl.multiple_of(head * HD, HD), HD)

    load_pairs = [
        (k_hbm, k_all.at[0]),
        (q_hbm, q_all.at[0]),
        (v_hbm, v_all.at[0]),
        (kb_hbm, kb_ref),
        (w_hbm, w_own),
        (g_hbm, g_full.at[:, my_columns]),
        (w_hbm.at[:, my_columns], w_col.at[my_columns, :]),
    ]
    loads = [
        pltpu.make_async_copy(source, target, load_sem.at[place])
        for place, (source, target) in enumerate(load_pairs)
    ]
    for load in loads:
        load.start()

    row, col = seq // ROW, lax.rem(seq, ROW)
    core = lax.rem(head, 2)
    last = ROW - 1
    in_row = [dist for dist in dists if dist < ROW]
    four = 4 in in_row
    barrier = pltpu.get_barrier_semaphore()

    def greet(peer_seq, peer_head, semaphore=barrier):
        pl.semaphore_signal(
            semaphore, inc=1, device_id=(peer_seq, peer_head), device_id_type=MESH
        )

    @pl.when(col < last)
    def _():
        greet(seq + 1, head)

    @pl.when(col > 0)
    def _():
        greet(seq - 1, head)

    @pl.when(col == 0)
    def _():
        greet(seq + last, head)

    @pl.when(col < last - 1)
    def _():
        greet(seq + 2, head)

    @pl.when(col < 2)
    def _():
        greet(seq + (last - 1), head)

    if four:

        @pl.when(col < 2)
        def _():
            greet(lax.rem(seq + (n_seq - 2), n_seq), head)

    rows_apart = sorted({ROW % n_seq, -ROW % n_seq})
    near_head = [head + 1 - 2 * core]
    if n_head == 8:
        near_head += [lax.rem(head + 2, n_head), lax.rem(head + (n_head - 2), n_head)]
    for apart in rows_apart:
        greet(lax.rem(seq + apart, n_seq), head)
    for peer in near_head:
        greet(seq, peer)
    expected = len(rows_apart) + len(near_head) + 3
    expected = expected - (last - col) // last - (last - col) // (last - 1)
    expected = expected + (2 if four else 1) * (col // (last - 1))
    pl.semaphore_wait(barrier, expected)

    @pl.when(col == last)
    def _():
        greet(seq - last, head, ready_sems.at[0])

    @pl.when(col > last - 2)
    def _():
        greet(seq - (last - 1), head, ready_sems.at[1])

    @pl.when(col > 1)
    def _():
        greet(seq - 2, head, ready_sems.at[2])

    where = (seq, head, n_seq, seq_send, seq_recv)
    keys_in = SeqCopies(0, dists, k_all, 1, *where)
    values_in = SeqCopies(1, dists, v_all, 1, *where)
    askers_in = SeqCopies(2, dists, q_all, -1, *where)
    grads_in = SeqCopies(3, dists, g_all, -1, *where, straight=True)
    out_gather = HeadGather(0, g_hbm, g_full, seq, head, n_head, head_send, head_recv)
    attn_gather = HeadGather(
        1, a_full.at[:, my_columns], a_full, seq, head, n_head, head_send, head_recv
    )
    w_copies = []
    for delta in range(1, n_head):
        peer = lax.rem(head + delta, n_head)
        w_copies.append(
            pltpu.make_async_remote_copy(
                src_ref=w_hbm.at[:, pl.ds(pl.multiple_of(peer * HD, HD), HD)],
                dst_ref=w_col.at[my_columns, :],
                send_sem=w_send.at[delta - 1],
                recv_sem=w_recv.at[delta - 1],
                device_id=(seq, peer),
                device_id_type=MESH,
            )
        )

    then = [("s", 4)] if four else []
    two = ("w", 2)
    out_gather.start()
    loads[0].wait()
    keys_in.do(("s", ROW))
    keys_in.when(0, last - 1, ("s", 1))
    loads[1].wait()
    askers_in.do(("s", ROW))
    askers_in.when(1, last, ("s", 1))
    askers_in.when(2, last, ("s", 2))
    loads[2].wait()
    values_in.do(("s", ROW))

    @pl.when(col < last - 1)
    def _():
        pl.semaphore_wait(ready_sems.at[2], 1)
        keys_in.do(("s", 2))

    values_in.when(0, last - 1, ("s", 1))
    values_in.when(0, last - 2, ("s", 2))

    keys_in.do(("w", ROW), ("s", 2 * ROW))
    keys_in.when(last, last, ("s", 1))
    keys_in.when(last - 1, last, ("s", 2))
    askers_in.do(("w", ROW), ("s", 2 * ROW))
    out_gather.middle()
    values_in.do(("w", ROW), ("s", 2 * ROW))
    values_in.when(last, last, ("s", 1))
    values_in.when(last - 1, last, ("s", 2))
    keys_in.when(2, last, two, *then)
    askers_in.when(0, last - 2, two)
    askers_in.when(2, last - 2, *then)
    out_gather.late()
    for load in loads[3:]:
        load.wait()
    out_gather.end()
    g_own = dot_nt(g_full[...], w_own[...]).astype(jnp.bfloat16)
    for block in range(nb):
        g_all[0, block] = g_own[block * BLOCK : (block + 1) * BLOCK]
    keys_in.do(("w", 2 * ROW), ("s", 4 * ROW))
    askers_in.do(("w", 2 * ROW), ("s", 4 * ROW))
    grads_in.do(("s", ROW))
    grads_in.when(1, last, ("s", 1))
    grads_in.when(2, last, ("s", 2))
    grads_in.do(("s", 2 * ROW))
    for copy in w_copies:
        copy.start()
    values_in.when(2, last, two, *then)
    values_in.do(("w", 2 * ROW), ("s", 4 * ROW))

    @pl.when(col == 0)
    def _():
        pl.semaphore_wait(ready_sems.at[0], 1)
        askers_in.do(("s", 1))

    @pl.when(col < 2)
    def _():
        pl.semaphore_wait(ready_sems.at[1], 1)
        askers_in.do(("s", 2))

    askers_in.when(last - 1, last, two, *then)
    grads_in.do(("w", ROW))
    grads_in.when(0, 0, ("s", 1))
    grads_in.when(0, 1, ("s", 2))
    grads_in.do(("w", 2 * ROW), ("s", 4 * ROW))
    grads_in.do(two)
    grads_in.when(2, last, *then)
    keys_in.when(0, 1, two, *then)
    askers_in.when(0, 1, *then)
    values_in.when(0, 1, two, *then)
    grads_in.when(0, 1, *then)
    keys_in.do(("w", 1), ("w", 4 * ROW))
    if four:
        keys_in.do(("w", 4))

    near = [2**power for power in range(LEVELS) if 2**power < nb]
    far = [(dist, 1 + place) for place, dist in enumerate(dists)]
    count = 1 + len(near) + len(far)
    width = count * BLOCK
    scaling = HD ** (-0.5)

    def gathered(buffer, block, sign):
        pieces = [buffer[0, block]]
        for stride in near:
            other = block - sign * stride
            pieces.append(buffer[0, other] if 0 <= other < nb else buffer[1, other % nb])
        for _, slot in far:
            pieces.append(buffer[slot, block])
        return jnp.concatenate(pieces, axis=0)

    lanes = lax.broadcasted_iota(jnp.int32, (1, width), 1)
    levels = lanes // BLOCK
    rows = lax.broadcasted_iota(jnp.int32, (BLOCK, width), 0)
    columns = lax.broadcasted_iota(jnp.int32, (BLOCK, width), 1)
    earlier = columns <= rows
    later = (columns >= rows) | (columns >= BLOCK)

    kept = []
    for block in range(nb):
        scores = dot_nt(q_all[0, block], gathered(k_all, block, 1)) * scaling
        flags = jnp.zeros((1, width), jnp.int32)
        for level in range(count - 1):
            flags = jnp.where(levels == level + 1, kb_ref[block : block + 1, level : level + 1], flags)
        allowed = (flags >= 0) & ((columns >= BLOCK) | earlier)
        scores = jnp.where(allowed, scores, -BIG)
        highest = jnp.max(scores, axis=1, keepdims=True)
        powers = jnp.exp(scores - highest)
        total = jnp.sum(powers, axis=1, keepdims=True)
        probs = powers * (1.0 / total)
        log_total = highest + jnp.log(total)
        kept.append((probs, log_total))

    values_in.do(("w", 1), ("w", 4 * ROW))
    if four:
        values_in.do(("w", 4))

    stat_lane = lax.broadcasted_iota(jnp.int32, (BLOCK, HD), 1)
    stats = jnp.zeros((BLOCK, HD), jnp.float32)
    inners = []
    for block in range(nb):
        probs, log_total = kept[block]
        attn = dot_nn(probs.astype(jnp.bfloat16), gathered(v_all, block, 1)).astype(jnp.bfloat16)
        a_full[block * BLOCK : (block + 1) * BLOCK, my_columns] = attn
        grads = g_all[0, block]
        inner = jnp.sum(grads.astype(jnp.float32) * attn.astype(jnp.float32), axis=1, keepdims=True)
        stats = jnp.where(stat_lane == block, log_total, stats)
        stats = jnp.where(stat_lane == nb + block, inner, stats)
        inners.append(inner)
    turned = jnp.concatenate([stats, stats], axis=0).T[0 : 2 * nb]
    stat_mine[0] = turned
    for level in range(count - 1):
        stat_mine[1 + level, 0:nb] = jnp.where(
            kb_ref[:, level : level + 1] >= 0, turned[0:nb], BIG
        )
        stat_mine[1 + level, nb : 2 * nb] = turned[nb : 2 * nb]
    first_far = 1 + len(near)
    stat_copies = []
    for number, (dist, slot) in enumerate(far):
        low = 1 if dist == 1 else first_far + number
        high = first_far + number + 1
        stat_copies.append(
            pltpu.make_async_remote_copy(
                src_ref=stat_mine.at[low:high],
                dst_ref=stat_got.at[low:high],
                send_sem=stat_send.at[number],
                recv_sem=stat_recv.at[number],
                device_id=(lax.rem(seq + (n_seq - dist), n_seq), head),
                device_id_type=MESH,
            )
        )
    for copy in reversed(stat_copies):
        copy.start()
    attn_gather.start()

    for block in range(nb):
        probs, _ = kept[block]
        grad_probs = dot_nt(g_all[0, block], gathered(v_all, block, 1))
        grad_scores = (probs * (grad_probs - inners[block]) * scaling).astype(jnp.bfloat16)
        dq_ref[block] = dot_nn(grad_scores, gathered(k_all, block, 1)).astype(jnp.bfloat16)
        if block == nb // 2:
            attn_gather.middle()

    for tensor in (askers_in, grads_in):
        tensor.do(("w", 1), ("w", 4 * ROW))
        if four:
            tensor.do(("w", 4))
    attn_gather.late()
    for copy in stat_copies:
        copy.wait_recv()

    half = lax.broadcasted_iota(jnp.int32, (1, 2 * BLOCK), 1) < BLOCK
    for block in range(nb):
        sources = [(stat_mine, 0, block)]
        for number, stride in enumerate(near):
            other = block + stride
            inside = other < nb
            sources.append((stat_mine if inside else stat_got, 1 + number, other % nb))
        for number in range(len(far)):
            sources.append((stat_got, first_far + number, block))

        def stat_row(offset):
            pieces = []
            for index in range(0, count, 2):
                ref, level, line = sources[index]
                piece = ref[level, offset + line : offset + line + 1, :]
                if index + 1 < count:
                    ref, level, line = sources[index + 1]
                    piece = jnp.where(half, piece, ref[level, offset + line : offset + line + 1, :])
                else:
                    piece = piece[:, 0:BLOCK]
                pieces.append(piece)
            return jnp.concatenate(pieces, axis=1)

        askers = gathered(q_all, block, -1)
        grads = gathered(g_all, block, -1)
        scores = dot_nt(k_all[0, block], askers) * scaling
        probs = jnp.exp(jnp.where(later, scores - stat_row(0), -BIG))
        dv_ref[block] = dot_nn(probs.astype(jnp.bfloat16), grads).astype(jnp.bfloat16)
        grad_probs = dot_nt(v_all[0, block], grads)
        grad_scores = (probs * (grad_probs - stat_row(nb)) * scaling).astype(jnp.bfloat16)
        dk_ref[block] = dot_nn(grad_scores, askers).astype(jnp.bfloat16)

    for copy in w_copies:
        copy.wait_recv()
    attn_gather.end()
    mixed_ref[...] = dot_nn(a_full[...], w_col[...]).astype(jnp.bfloat16)

    for part in (keys_in, values_in, askers_in, grads_in, out_gather, attn_gather):
        part.finish()
    for copy in w_copies + stat_copies:
        copy.wait_send()


def put_out(*refs):
    count = len(refs) // 2
    for source, target in zip(refs[:count], refs[count:]):
        target[...] = source[...]


def per_device(queries, key_rows, value_rows, key_blocks, out_weight, grad_out):
    n_seq, n_head = lax.axis_size("seq"), lax.axis_size("head")
    rows = queries.shape[0]
    width = out_weight.shape[1]
    nb = rows // BLOCK
    dists = [2**power // nb for power in range(LEVELS) if nb <= 2**power < nb * n_seq]
    blocked = (nb, BLOCK, HD)
    slots = (1 + len(dists),) + blocked
    near = [2**power for power in range(LEVELS) if 2**power < nb]
    count = 1 + len(near) + len(dists)
    vmem = pl.BlockSpec(memory_space=pltpu.VMEM)
    hbm = pl.BlockSpec(memory_space=pltpu.HBM)
    seq_sems = pltpu.SemaphoreType.DMA((4 * len(dists),))
    results = pl.pallas_call(
        functools.partial(kernel, n_seq, n_head, dists),
        out_shape=[jax.ShapeDtypeStruct((rows, HD), jnp.bfloat16)]
        + [jax.ShapeDtypeStruct(blocked, jnp.bfloat16)] * 3,
        in_specs=[hbm] * 6,
        out_specs=[vmem] * 4,
        scratch_shapes=[pltpu.VMEM(slots, jnp.bfloat16)] * 4
        + [
            pltpu.VMEM((rows, width), jnp.bfloat16),
            pltpu.VMEM((HD, width), jnp.bfloat16),
            pltpu.VMEM((width, HD), jnp.bfloat16),
            pltpu.VMEM((rows, width), jnp.bfloat16),
            pltpu.VMEM((count, 2 * nb, HD), jnp.float32),
            pltpu.VMEM((count, 2 * nb, HD), jnp.float32),
            pltpu.VMEM(key_blocks.shape, jnp.int32),
            seq_sems,
            seq_sems,
            pltpu.SemaphoreType.DMA((14,)),
            pltpu.SemaphoreType.DMA((14,)),
            pltpu.SemaphoreType.DMA((n_head - 1,)),
            pltpu.SemaphoreType.DMA((n_head - 1,)),
            pltpu.SemaphoreType.DMA((len(dists),)),
            pltpu.SemaphoreType.DMA((len(dists),)),
            pltpu.SemaphoreType.DMA((7,)),
            pltpu.SemaphoreType.REGULAR((3,)),
        ],
        compiler_params=pltpu.CompilerParams(
            collective_id=0, has_side_effects=True, vmem_limit_bytes=20 * 2**20
        ),
        name="attention",
    )(
        *[
            pltpu.with_memory_space_constraint(array, pltpu.HBM)
            for array in (
                queries.reshape(blocked),
                key_rows.reshape(blocked),
                value_rows.reshape(blocked),
                key_blocks,
                out_weight,
                grad_out,
            )
        ]
    )
    results = pl.pallas_call(
        put_out,
        out_shape=[jax.ShapeDtypeStruct(result.shape, result.dtype) for result in results],
        in_specs=[vmem] * 4,
        out_specs=[vmem] * 4,
        compiler_params=pltpu.CompilerParams(vmem_limit_bytes=8 * 2**20),
        name="put_out",
    )(*results)
    return tuple(result.reshape(rows, HD) for result in results)


def solution(mesh):
    in_specs = (
        P("seq", "head"),
        P("seq", "head"),
        P("seq", "head"),
        P("seq", None),
        P("head", None),
        P("seq", "head"),
    )
    out_specs = (P("seq", "head"), P("seq", "head"), P("seq", "head"), P("seq", "head"))
    return jax.shard_map(
        per_device, mesh=mesh, in_specs=in_specs, out_specs=out_specs, check_vma=False
    )
```

```python
import functools

import jax
import jax.numpy as jnp
from jax import lax
from jax.experimental import pallas as pl
from jax.experimental.pallas import tpu as pltpu
from jax.sharding import PartitionSpec as P

HD = 128
BLOCK = 64
LEVELS = 9
ROW = 8
MESH = pl.DeviceIdType.MESH
BIG = 1e30


def dot_nt(a, b):
    return lax.dot_general(a, b, (((1,), (1,)), ((), ())), preferred_element_type=jnp.float32)


def dot_nn(a, b):
    return lax.dot_general(a, b, (((1,), (0,)), ((), ())), preferred_element_type=jnp.float32)


class SeqCopies:
    def __init__(self, number, dists, buffer, sign, seq, head, n_seq, send, recv, own, straight=False):
        self.dists, self.ahead = dists, sign > 0
        row, self.col = seq // ROW, lax.rem(seq, ROW)
        self.slot = {dist: 1 + place for place, dist in enumerate(dists)}
        in_row = lambda hop: row * ROW + lax.rem(self.col + (sign * hop + ROW), ROW)
        jump = lambda hop: lax.rem(seq + (sign * hop + n_seq), n_seq)
        base = number * len(dists)

        def copy(source, target, place, device):
            return pltpu.make_async_remote_copy(
                src_ref=source,
                dst_ref=buffer.at[target],
                send_sem=send.at[base + place],
                recv_sem=recv.at[base + place],
                device_id=(device, head),
                device_id_type=MESH,
            )

        self.copies, self.firsts = {}, {}
        for place, dist in enumerate(dists):
            slot = self.slot[dist]
            if dist <= 2:
                source, device = self.slot[ROW], in_row(dist)
            elif dist == ROW:
                source, device = 0, jump(ROW)
            elif dist == 2 * ROW and straight:
                source, device = 0, jump(2 * ROW)
            elif dist == 2 * ROW:
                source, device = self.slot[ROW], jump(ROW)
            else:
                source, device = self.slot[dist // 2], jump(dist // 2)
            self.copies[dist] = copy(buffer.at[source], slot, place, device)
            self.firsts[dist] = copy(own, slot, place, device)

    def when(self, low, high, *steps):
        @pl.when((self.col >= low) & (self.col <= high))
        def _():
            self.do(*steps)

    def do(self, *steps):
        for step, dist in steps:
            if dist in self.copies:
                copy = (self.firsts if step == "o" else self.copies)[dist]
                copy.wait_recv() if step == "w" else copy.start()

    def finish(self):
        for dist in self.dists:
            self.copies[dist].wait_send()


class HeadGather:
    def __init__(self, number, own, buffer, seq, head, n_head, send, recv):
        core = lax.rem(head, 2)
        partner = head + 1 - 2 * core
        toward = 2 - 4 * core
        wrap = lambda value: lax.rem(value + 2 * n_head, n_head)

        def columns(who):
            return buffer.at[:, pl.ds(pl.multiple_of(who * HD, HD), HD)]

        def copy(place, who, device, source=None):
            return pltpu.make_async_remote_copy(
                src_ref=columns(who) if source is None else source,
                dst_ref=columns(who),
                send_sem=send.at[7 * number + place],
                recv_sem=recv.at[7 * number + place],
                device_id=(seq, device),
                device_id_type=MESH,
            )

        self.first = [copy(0, head, partner, own)]
        self.relays, self.passes, self.last = [], [], []
        if n_head == 8:
            self.first.append(copy(1, head, wrap(head + toward), own))
            self.first.append(copy(2, head, wrap(head - toward), own))
            self.first.append(copy(3, head, wrap(head + 4), own))
            self.relays.append(self.first[3])
            self.passes.append(copy(4, wrap(head - toward), partner))
            self.passes.append(copy(5, wrap(head + toward), partner))
            self.last.append(copy(6, wrap(head + 4), partner))

    def start(self):
        for copy in reversed(self.first):
            copy.start()

    def middle(self):
        if self.relays:
            self.first[1].wait_recv()
            self.passes[0].start()
            self.first[2].wait_recv()
            self.passes[1].start()

    def late(self):
        if self.relays:
            self.relays[0].wait_recv()
            self.last[0].start()

    def end(self):
        for copy in self.first[:1] + self.passes + self.last:
            copy.wait_recv()

    def finish(self):
        for copy in self.first + self.passes + self.last:
            copy.wait_send()


def kernel(
    n_seq, n_head, dists,
    q_hbm, k_hbm, v_hbm, kb_hbm, w_hbm, g_hbm,
    mixed_ref, dq_ref, dk_ref, dv_ref,
    k_all, v_all, q_all, g_all, g_full, w_own, w_col, a_full, stat_mine, stat_got, kb_ref,
    seq_send, seq_recv, head_send, head_recv, w_send, w_recv, stat_send, stat_recv, load_sem, ready_sems,
):
    seq = lax.axis_index("seq")
    head = lax.axis_index("head")
    nb = q_hbm.shape[0]
    my_columns = pl.ds(pl.multiple_of(head * HD, HD), HD)

    load_pairs = [
        (k_hbm, k_all.at[0]),
        (q_hbm, q_all.at[0]),
        (v_hbm, v_all.at[0]),
        (kb_hbm, kb_ref),
        (w_hbm, w_own),
        (g_hbm, g_full.at[:, my_columns]),
        (w_hbm.at[:, my_columns], w_col.at[my_columns, :]),
    ]
    loads = [
        pltpu.make_async_copy(source, target, load_sem.at[place])
        for place, (source, target) in enumerate(load_pairs)
    ]
    for load in loads:
        load.start()

    row, col = seq // ROW, lax.rem(seq, ROW)
    core = lax.rem(head, 2)
    last = ROW - 1
    in_row = [dist for dist in dists if dist < ROW]
    four = 4 in in_row
    barrier = pltpu.get_barrier_semaphore()

    def greet(peer_seq, peer_head, semaphore=barrier):
        pl.semaphore_signal(
            semaphore, inc=1, device_id=(peer_seq, peer_head), device_id_type=MESH
        )

    @pl.when(col < last)
    def _():
        greet(seq + 1, head)

    @pl.when(col > 0)
    def _():
        greet(seq - 1, head)

    @pl.when(col == 0)
    def _():
        greet(seq + last, head)

    @pl.when(col < last - 1)
    def _():
        greet(seq + 2, head)

    @pl.when(col < 2)
    def _():
        greet(seq + (last - 1), head)

    if four:

        @pl.when(col < 2)
        def _():
            greet(lax.rem(seq + (n_seq - 2), n_seq), head)

    rows_apart = sorted({ROW % n_seq, -ROW % n_seq})
    near_head = [head + 1 - 2 * core]
    if n_head == 8:
        near_head += [lax.rem(head + hop, n_head) for hop in (2, 4, 6)]
    for apart in rows_apart:
        greet(lax.rem(seq + apart, n_seq), head)
    for peer in near_head:
        greet(seq, peer)
    expected = len(rows_apart) + len(near_head) + 3
    expected = expected - (last - col) // last - (last - col) // (last - 1)
    expected = expected + (2 if four else 1) * (col // (last - 1))
    pl.semaphore_wait(barrier, expected)

    @pl.when(col == last)
    def _():
        greet(seq - last, head, ready_sems.at[0])

    @pl.when(col > last - 2)
    def _():
        greet(seq - (last - 1), head, ready_sems.at[1])

    @pl.when(col > 1)
    def _():
        greet(seq - 2, head, ready_sems.at[2])

    where = (seq, head, n_seq, seq_send, seq_recv)
    keys_in = SeqCopies(0, dists, k_all, 1, *where, k_hbm)
    values_in = SeqCopies(1, dists, v_all, 1, *where, v_hbm)
    askers_in = SeqCopies(2, dists, q_all, -1, *where, q_hbm)
    grads_in = SeqCopies(3, dists, g_all, -1, *where, g_all.at[0], straight=True)
    out_gather = HeadGather(0, g_hbm, g_full, seq, head, n_head, head_send, head_recv)
    attn_gather = HeadGather(
        1, a_full.at[:, my_columns], a_full, seq, head, n_head, head_send, head_recv
    )
    w_copies = []
    for delta in range(1, n_head):
        peer = lax.rem(head + delta, n_head)
        w_copies.append(
            pltpu.make_async_remote_copy(
                src_ref=w_hbm.at[:, pl.ds(pl.multiple_of(peer * HD, HD), HD)],
                dst_ref=w_col.at[my_columns, :],
                send_sem=w_send.at[delta - 1],
                recv_sem=w_recv.at[delta - 1],
                device_id=(seq, peer),
                device_id_type=MESH,
            )
        )

    then = [("s", 4)] if four else []
    two = ("w", 2)
    keys_in.do(("o", ROW))
    keys_in.when(0, last - 1, ("o", 1))
    askers_in.do(("o", ROW))
    askers_in.when(1, last, ("o", 1))
    askers_in.when(2, last, ("o", 2))
    out_gather.start()
    values_in.do(("o", ROW))

    @pl.when(col < last - 1)
    def _():
        pl.semaphore_wait(ready_sems.at[2], 1)
        keys_in.do(("o", 2))

    values_in.when(0, last - 1, ("o", 1))
    values_in.when(0, last - 2, ("o", 2))

    keys_in.do(("w", ROW), ("s", 2 * ROW))
    keys_in.when(last, last, ("s", 1))
    keys_in.when(last - 1, last, ("s", 2))
    askers_in.do(("w", ROW), ("s", 2 * ROW))
    out_gather.middle()
    values_in.do(("w", ROW), ("s", 2 * ROW))
    values_in.when(last, last, ("s", 1))
    values_in.when(last - 1, last, ("s", 2))
    keys_in.when(2, last, two, *then)
    askers_in.when(0, last - 2, two)
    askers_in.when(2, last - 2, *then)
    out_gather.late()
    for load in loads:
        load.wait()
    out_gather.end()
    g_own = dot_nt(g_full[...], w_own[...]).astype(jnp.bfloat16)
    for block in range(nb):
        g_all[0, block] = g_own[block * BLOCK : (block + 1) * BLOCK]
    keys_in.do(("w", 2 * ROW), ("s", 4 * ROW))
    askers_in.do(("w", 2 * ROW), ("s", 4 * ROW))
    grads_in.do(("o", ROW))
    grads_in.when(1, last, ("o", 1))
    grads_in.when(2, last, ("o", 2))
    grads_in.do(("o", 2 * ROW))
    for copy in w_copies:
        copy.start()
    values_in.when(2, last, two, *then)
    values_in.do(("w", 2 * ROW), ("s", 4 * ROW))

    @pl.when(col == 0)
    def _():
        pl.semaphore_wait(ready_sems.at[0], 1)
        askers_in.do(("s", 1))

    @pl.when(col < 2)
    def _():
        pl.semaphore_wait(ready_sems.at[1], 1)
        askers_in.do(("s", 2))

    askers_in.when(last - 1, last, two, *then)
    grads_in.do(("w", ROW))
    grads_in.when(0, 0, ("s", 1))
    grads_in.when(0, 1, ("s", 2))
    keys_in.when(0, 1, two, *then)
    askers_in.when(0, 1, *then)
    values_in.when(0, 1, two, *then)
    grads_in.do(("w", 2 * ROW), ("s", 4 * ROW))
    grads_in.do(two)
    grads_in.when(2, last, *then)
    grads_in.when(0, 1, *then)
    keys_in.do(("w", 1), ("w", 4 * ROW))
    if four:
        keys_in.do(("w", 4))

    near = [2**power for power in range(LEVELS) if 2**power < nb]
    far = [(dist, 1 + place) for place, dist in enumerate(dists)]
    count = 1 + len(near) + len(far)
    width = count * BLOCK
    scaling = HD ** (-0.5)

    def gathered(buffer, block, sign):
        pieces = [buffer[0, block]]
        for stride in near:
            other = block - sign * stride
            pieces.append(buffer[0, other] if 0 <= other < nb else buffer[1, other % nb])
        for _, slot in far:
            pieces.append(buffer[slot, block])
        return jnp.concatenate(pieces, axis=0)

    lanes = lax.broadcasted_iota(jnp.int32, (1, width), 1)
    levels = lanes // BLOCK
    rows = lax.broadcasted_iota(jnp.int32, (BLOCK, width), 0)
    columns = lax.broadcasted_iota(jnp.int32, (BLOCK, width), 1)
    earlier = columns <= rows
    later = (columns >= rows) | (columns >= BLOCK)

    kept = []
    for block in range(nb):
        scores = dot_nt(q_all[0, block], gathered(k_all, block, 1)) * scaling
        flags = jnp.zeros((1, width), jnp.int32)
        for level in range(count - 1):
            flags = jnp.where(levels == level + 1, kb_ref[block : block + 1, level : level + 1], flags)
        allowed = (flags >= 0) & ((columns >= BLOCK) | earlier)
        scores = jnp.where(allowed, scores, -BIG)
        highest = jnp.max(scores, axis=1, keepdims=True)
        powers = jnp.exp(scores - highest)
        total = jnp.sum(powers, axis=1, keepdims=True)
        probs = powers * (1.0 / total)
        log_total = highest + jnp.log(total)
        kept.append((probs, log_total))

    values_in.do(("w", 1), ("w", 4 * ROW))
    if four:
        values_in.do(("w", 4))

    stat_lane = lax.broadcasted_iota(jnp.int32, (BLOCK, HD), 1)
    stats = jnp.zeros((BLOCK, HD), jnp.float32)
    inners = []
    for block in range(nb):
        probs, log_total = kept[block]
        attn = dot_nn(probs.astype(jnp.bfloat16), gathered(v_all, block, 1)).astype(jnp.bfloat16)
        a_full[block * BLOCK : (block + 1) * BLOCK, my_columns] = attn
        grads = g_all[0, block]
        inner = jnp.sum(grads.astype(jnp.float32) * attn.astype(jnp.float32), axis=1, keepdims=True)
        stats = jnp.where(stat_lane == block, log_total, stats)
        stats = jnp.where(stat_lane == nb + block, inner, stats)
        inners.append(inner)
    attn_gather.start()
    turned = jnp.concatenate([stats, stats], axis=0).T[0 : 2 * nb]
    stat_mine[0] = turned
    for level in range(count - 1):
        stat_mine[1 + level, 0:nb] = jnp.where(
            kb_ref[:, level : level + 1] >= 0, turned[0:nb], BIG
        )
        stat_mine[1 + level, nb : 2 * nb] = turned[nb : 2 * nb]
    first_far = 1 + len(near)
    stat_copies = []
    for number, (dist, slot) in enumerate(far):
        low = 1 if dist == 1 else first_far + number
        high = first_far + number + 1
        stat_copies.append(
            pltpu.make_async_remote_copy(
                src_ref=stat_mine.at[low:high],
                dst_ref=stat_got.at[low:high],
                send_sem=stat_send.at[number],
                recv_sem=stat_recv.at[number],
                device_id=(lax.rem(seq + (n_seq - dist), n_seq), head),
                device_id_type=MESH,
            )
        )
    for copy in reversed(stat_copies):
        copy.start()

    for block in range(nb):
        probs, _ = kept[block]
        grad_probs = dot_nt(g_all[0, block], gathered(v_all, block, 1))
        grad_scores = (probs * (grad_probs - inners[block]) * scaling).astype(jnp.bfloat16)
        dq_ref[block] = dot_nn(grad_scores, gathered(k_all, block, 1)).astype(jnp.bfloat16)

    attn_gather.middle()
    attn_gather.late()
    for tensor in (askers_in, grads_in):
        tensor.do(("w", 1), ("w", 4 * ROW))
        if four:
            tensor.do(("w", 4))
    drafts = []
    for block in range(nb):
        askers = gathered(q_all, block, -1)
        grads = gathered(g_all, block, -1)
        drafts.append(
            (dot_nt(k_all[0, block], askers) * scaling, dot_nt(v_all[0, block], grads))
        )
    for copy in w_copies:
        copy.wait_recv()
    attn_gather.end()
    mixed_ref[...] = dot_nn(a_full[...], w_col[...]).astype(jnp.bfloat16)
    for copy in stat_copies:
        copy.wait_recv()

    half = lax.broadcasted_iota(jnp.int32, (1, 2 * BLOCK), 1) < BLOCK
    for block in range(nb):
        sources = [(stat_mine, 0, block)]
        for number, stride in enumerate(near):
            other = block + stride
            inside = other < nb
            sources.append((stat_mine if inside else stat_got, 1 + number, other % nb))
        for number in range(len(far)):
            sources.append((stat_got, first_far + number, block))

        def stat_row(offset):
            pieces = []
            for index in range(0, count, 2):
                ref, level, line = sources[index]
                piece = ref[level, offset + line : offset + line + 1, :]
                if index + 1 < count:
                    ref, level, line = sources[index + 1]
                    piece = jnp.where(half, piece, ref[level, offset + line : offset + line + 1, :])
                else:
                    piece = piece[:, 0:BLOCK]
                pieces.append(piece)
            return jnp.concatenate(pieces, axis=1)

        askers = gathered(q_all, block, -1)
        grads = gathered(g_all, block, -1)
        scores, grad_probs = drafts[block]
        probs = jnp.exp(jnp.where(later, scores - stat_row(0), -BIG))
        dv_ref[block] = dot_nn(probs.astype(jnp.bfloat16), grads).astype(jnp.bfloat16)
        grad_scores = (probs * (grad_probs - stat_row(nb)) * scaling).astype(jnp.bfloat16)
        dk_ref[block] = dot_nn(grad_scores, askers).astype(jnp.bfloat16)

    for part in (keys_in, values_in, askers_in, grads_in, out_gather, attn_gather):
        part.finish()
    for copy in w_copies + stat_copies:
        copy.wait_send()


def put_out(*refs):
    count = len(refs) // 2
    for source, target in zip(refs[:count], refs[count:]):
        target[...] = source[...]


def per_device(queries, key_rows, value_rows, key_blocks, out_weight, grad_out):
    n_seq, n_head = lax.axis_size("seq"), lax.axis_size("head")
    rows = queries.shape[0]
    width = out_weight.shape[1]
    nb = rows // BLOCK
    dists = [2**power // nb for power in range(LEVELS) if nb <= 2**power < nb * n_seq]
    blocked = (nb, BLOCK, HD)
    slots = (1 + len(dists),) + blocked
    near = [2**power for power in range(LEVELS) if 2**power < nb]
    count = 1 + len(near) + len(dists)
    vmem = pl.BlockSpec(memory_space=pltpu.VMEM)
    hbm = pl.BlockSpec(memory_space=pltpu.HBM)
    seq_sems = pltpu.SemaphoreType.DMA((4 * len(dists),))
    results = pl.pallas_call(
        functools.partial(kernel, n_seq, n_head, dists),
        out_shape=[jax.ShapeDtypeStruct((rows, HD), jnp.bfloat16)]
        + [jax.ShapeDtypeStruct(blocked, jnp.bfloat16)] * 3,
        in_specs=[hbm] * 6,
        out_specs=[vmem] * 4,
        scratch_shapes=[pltpu.VMEM(slots, jnp.bfloat16)] * 4
        + [
            pltpu.VMEM((rows, width), jnp.bfloat16),
            pltpu.VMEM((HD, width), jnp.bfloat16),
            pltpu.VMEM((width, HD), jnp.bfloat16),
            pltpu.VMEM((rows, width), jnp.bfloat16),
            pltpu.VMEM((count, 2 * nb, HD), jnp.float32),
            pltpu.VMEM((count, 2 * nb, HD), jnp.float32),
            pltpu.VMEM(key_blocks.shape, jnp.int32),
            seq_sems,
            seq_sems,
            pltpu.SemaphoreType.DMA((14,)),
            pltpu.SemaphoreType.DMA((14,)),
            pltpu.SemaphoreType.DMA((n_head - 1,)),
            pltpu.SemaphoreType.DMA((n_head - 1,)),
            pltpu.SemaphoreType.DMA((len(dists),)),
            pltpu.SemaphoreType.DMA((len(dists),)),
            pltpu.SemaphoreType.DMA((7,)),
            pltpu.SemaphoreType.REGULAR((3,)),
        ],
        compiler_params=pltpu.CompilerParams(
            collective_id=0, has_side_effects=True, vmem_limit_bytes=20 * 2**20
        ),
        name="attention",
    )(
        *[
            pltpu.with_memory_space_constraint(array, pltpu.HBM)
            for array in (
                queries.reshape(blocked),
                key_rows.reshape(blocked),
                value_rows.reshape(blocked),
                key_blocks,
                out_weight,
                grad_out,
            )
        ]
    )
    results = pl.pallas_call(
        put_out,
        out_shape=[jax.ShapeDtypeStruct(result.shape, result.dtype) for result in results],
        in_specs=[vmem] * 4,
        out_specs=[vmem] * 4,
        compiler_params=pltpu.CompilerParams(vmem_limit_bytes=8 * 2**20),
        name="put_out",
    )(*results)
    return tuple(result.reshape(rows, HD) for result in results)


def solution(mesh):
    in_specs = (
        P("seq", "head"),
        P("seq", "head"),
        P("seq", "head"),
        P("seq", None),
        P("head", None),
        P("seq", "head"),
    )
    out_specs = (P("seq", "head"), P("seq", "head"), P("seq", "head"), P("seq", "head"))
    return jax.shard_map(
        per_device, mesh=mesh, in_specs=in_specs, out_specs=out_specs, check_vma=False
    )
```
